256 devices in a mesh: src: 64 (over y_hi, z, x), row: 4 (over y_lo, core).
Axes of the slice: x: 4, y: 4 (y_hi: 2, y_lo: 2; y = y_hi * 2 + y_lo), z: 8, core: 2. Of those that a mesh axis runs over, the one named last changes fastest.
Arguments:
- right_side: float32 [2, 8192, 16384], P(None, 'row', 'src'), may hold values from -6 to 6
- pivot_inverse: float32 [2, 2, 512, 512], P(None, None, 'src')
- ancestor_panel: float32 [2, 2, 4096, 512], P(None, None, ('row', 'src')), may hold values from -0.1875 to 0.1875
- ancestors: int32 [2, 4096], P(None, 'row'), may hold values from -1 to 2047, as said below
- pivot_block: int32 [2], replicated, may hold values from 0 to 15, as said below
Outputs:
- forward: float32 [2, 8192, 16384], P(None, 'row', 'src')
The draws below stay inside these ranges and needn't reach their ends.
Inputs may be any that keep to these rules, and one draw needn't show every extreme that they name: pivot_block holds 2 distinct blocks of 512 rows; one of them is always the last block. `ancestors`: for supernode k and row device r, slots r * 1024 to r * 1024 + 1023 hold distinct rising local rows of that device followed by -1 in the remaining slots; they never touch the pivot rows of supernodes 0 to k, and for k below 1 they include every pivot row of supernode k + 1 that lies on that device; for each supernode some row device fills all 1024 slots.
All inputs are finite; a program needn't handle non-finite values.
Results may differ from the reference program's by a relative error of at most 0.0001.
Values sent between devices are 32-bit elements; how exact they have to be, the bound alone decides.
No kernel may reach another device: no remote copies, remote signals or barrier semaphores. Data moves between devices by JAX's collectives and lax.ppermute only.
A program may use at most 128 MiB of HBM per device.

```python
import jax
import jax.numpy as jnp
from jax import lax

P_SIZE = 512
ROWS = 8192
AD = 1024
NODES = 2
R_LOC = 2048
COLS = 16384
N_ROW = 4


def chosen_blocks(key):
    last_block = ROWS // P_SIZE - 1
    others = jax.random.permutation(jax.random.fold_in(key, 7), last_block)[:NODES - 1].astype(jnp.int32)
    picked = jnp.concatenate([others, jnp.full((1,), last_block, jnp.int32)])
    order = jax.random.permutation(jax.random.fold_in(key, 8), NODES)
    return picked[order].astype(jnp.int32)


def draw_pivot_block(key, part):
    return chosen_blocks(key)


def device_slots(key, supernode, device, blocks):
    local_rows = jnp.arange(R_LOC, dtype=jnp.int32)
    row_block = (device * R_LOC + local_rows) // P_SIZE
    excluded = jnp.zeros((R_LOC,), bool)
    for earlier in range(supernode + 1):
        excluded = excluded | (row_block == blocks[earlier])
    if supernode + 1 < NODES:
        forced = row_block == blocks[supernode + 1]
        full_device = blocks[supernode + 1] // (R_LOC // P_SIZE)
    else:
        forced = jnp.zeros((R_LOC,), bool)
        full_device = (blocks[supernode] // (R_LOC // P_SIZE) + 1) % N_ROW
    noise_bits = jax.random.randint(jax.random.fold_in(key, 1), (R_LOC,), 0, 2 ** 16)
    scores = jnp.where(forced, local_rows - R_LOC, jnp.where(excluded, 2 ** 30 + local_rows, noise_bits * R_LOC + local_rows))
    ordering = jnp.argsort(scores, stable=True)[:AD].astype(jnp.int32)
    allowed = R_LOC - jnp.sum(excluded.astype(jnp.int32))
    drawn_count = jax.random.randint(jax.random.fold_in(key, 2), (), AD // 4, AD + 1)
    count_live = jnp.where(device == full_device, AD, jnp.minimum(drawn_count, allowed))
    slots = jnp.arange(AD, dtype=jnp.int32)
    keyed = jnp.sort(jnp.where(slots < count_live, ordering, R_LOC + slots))
    return jnp.where(keyed < R_LOC, keyed, -1).astype(jnp.int32)


def draw_ancestors(key, part):
    blocks = chosen_blocks(key)
    result = []
    for supernode in range(NODES):
        node_key = jax.random.fold_in(key, 100 + supernode)
        devices = jnp.arange(N_ROW, dtype=jnp.int32)
        filled = jax.vmap(lambda device: device_slots(jax.random.fold_in(node_key, device), supernode, device, blocks))(devices)
        result.append(filled.reshape(N_ROW * AD))
    return jnp.stack(result).astype(jnp.int32)


def draw_pivot_inverse(key, part):
    first_key, second_key, third_key = jax.random.split(jax.random.fold_in(key, 11), 3)
    lines = jnp.arange(P_SIZE)
    below = (lines[:, None] > lines[None, :]).astype(jnp.float32)
    entries = jax.random.normal(first_key, (NODES, 2, P_SIZE, P_SIZE), jnp.float32) * 0.7 / P_SIZE ** 0.5
    diag_real = jax.random.uniform(second_key, (NODES, P_SIZE), jnp.float32, 0.8, 1.2)
    diag_imag = jax.random.uniform(third_key, (NODES, P_SIZE), jnp.float32, -0.4, 0.4)
    eye = jnp.eye(P_SIZE, dtype=jnp.float32)
    real_part = entries[:, 0] * below + diag_real[:, :, None] * eye
    imag_part = entries[:, 1] * below + diag_imag[:, :, None] * eye
    return jnp.stack([real_part, imag_part], axis=1).astype(jnp.float32)


def level_of(own_key, extent, cuts, smallest, largest):
    level, own = 1.0, jax.random.fold_in(own_key, 6)
    for dim, parts in cuts:
        draws = jnp.exp(jax.random.uniform(jax.random.fold_in(own, dim), (parts,), jnp.float32, smallest / len(cuts), largest / len(cuts)))
        level = level * jnp.repeat(draws, extent[dim] // parts).reshape([-1 if axis == dim else 1 for axis in range(len(extent))])
    return level


def normal_values(stream_key, extent, width, bound, cuts=(), held_as=jnp.bfloat16):
    values = width * jax.random.normal(stream_key, extent, jnp.float32)
    if cuts:
        values = values * level_of(stream_key, extent, cuts, -0.22, 0.18)
    return jnp.clip(values, -bound, bound).astype(held_as)


def setup_inputs(seed: int = 0) -> dict:
    arg_keys = jax.random.split(jax.random.key(seed), 6)
    return {
        "right_side": normal_values(arg_keys[0], (2, ROWS, COLS), 1.0, 6.0, ((1, 4), (2, 64)), jnp.float32),
        "pivot_inverse": draw_pivot_inverse(jax.random.fold_in(arg_keys[5], 71), 0),
        "ancestor_panel": normal_values(arg_keys[2], (NODES, 2, N_ROW * AD, P_SIZE), (2 * P_SIZE) ** -0.5, 0.1875, ((2, 256),), jnp.float32),
        "ancestors": draw_ancestors(jax.random.fold_in(arg_keys[5], 71), 0),
        "pivot_block": draw_pivot_block(jax.random.fold_in(arg_keys[5], 71), 0),
    }


def complex_product(factor, operand):
    hint = lax.Precision.HIGHEST
    real_part = jnp.dot(factor[0], operand[0], precision=hint, preferred_element_type=jnp.float32) - jnp.dot(factor[1], operand[1], precision=hint, preferred_element_type=jnp.float32)
    imag_part = jnp.dot(factor[0], operand[1], precision=hint, preferred_element_type=jnp.float32) + jnp.dot(factor[1], operand[0], precision=hint, preferred_element_type=jnp.float32)
    return jnp.stack([real_part, imag_part])


def reference(right_side, pivot_inverse, ancestor_panel, ancestors, pivot_block):
    front_rows = right_side
    slots = jnp.arange(N_ROW * AD, dtype=jnp.int32)
    for supernode in range(NODES):
        offset = (pivot_block[supernode] * P_SIZE).astype(jnp.int32)
        pivot_part = lax.dynamic_slice_in_dim(front_rows, offset, P_SIZE, 1)
        solved = complex_product(pivot_inverse[supernode], pivot_part)
        front_rows = lax.dynamic_update_slice_in_dim(front_rows, solved, offset, 1)
        update = complex_product(ancestor_panel[supernode], solved)
        live_slots = ancestors[supernode] >= 0
        target = jnp.where(live_slots, (slots // AD) * R_LOC + ancestors[supernode], 0).astype(jnp.int32)
        front_rows = front_rows.at[:, target, :].add(-jnp.where(live_slots[None, :, None], update, 0.0))
    return front_rows
```

```python
import functools

import jax
import jax.numpy as jnp
import numpy as np
from jax import lax
from jax.experimental import pallas as pl
from jax.experimental.pallas import tpu as pltpu
from jax.sharding import Mesh, PartitionSpec as P


SIZES = {"yh": 2, "z": 8, "x": 4, "yl": 2, "c": 2}
SRC = ("yh", "z", "x")
ROW = ("yl", "c")
MIB = 1024 * 1024
cat = jnp.concatenate


def send(value, axis, shift):
    size = SIZES[axis]
    return lax.ppermute(value, axis, [(i, (i + shift) % size) for i in range(size)])


def ring_z(own):
    half = own.shape[0] // 2
    up1, down1 = send(own, "z", 1), send(own, "z", -1)
    up2, down2 = send(up1, "z", 1), send(down1, "z", -1)
    up3, down3 = send(up2, "z", 1), send(down2, "z", -1)
    up4, down4 = send(up3[:half], "z", 1), send(down3[half:], "z", -1)
    return [own, up1, down1, up2, down2, up3, down3, up4, down4]


def ring_z_short(own):
    half = own.shape[0] // 2
    up1, down1 = send(own, "z", 1), send(own, "z", -1)
    up2, down2 = send(own, "z", 2), send(own, "z", -2)
    up3, down3 = send(up2, "z", 1), send(down2, "z", -1)
    up4, down4 = send(up2[:half], "z", 2), send(down2[half:], "z", -2)
    return [own, up1, down1, up2, down2, up3, down3, up4, down4]


def ring_x(own):
    half = own.shape[0] // 2
    up1, down1 = send(own, "x", 1), send(own, "x", -1)
    up2, down2 = send(up1[:half], "x", 1), send(down1[half:], "x", -1)
    return [own, up1, down1, up2, down2]


Z_STEPS = [0, -1, 1, -2, 2, -3, 3]
X_STEPS = [0, -1, 1]


def offsets_a():
    block = [(dy, dx) for dx in (0, -1, 1, -2) for dy in (0, 1)]
    rows = [(dy, dz, dx) for dz in Z_STEPS for dy, dx in block]
    rows += [(dy, 4, dx) for dy, dx in block]
    return np.array(rows, np.int32)


def offsets_b():
    block = [(dy, dz) for dz in Z_STEPS + [4] for dy in (0, 1)]
    rows = [(dy, dz, dx) for dx in X_STEPS + [2] for dy, dz in block]
    return np.array(rows, np.int32)


def sources(offsets):
    yh, z, x = (lax.axis_index(a) for a in SRC)
    return (
        ((yh + offsets[:, 0]) % 2) * 32 + ((z + offsets[:, 1]) % 8) * 4 + (x + offsets[:, 2]) % 4
    ).astype(jnp.int32)


def from_owner(masked):
    core = lax.axis_index("c")
    both = masked + send(masked, "c", 1)
    mine = lax.dynamic_index_in_dim(both, core, 0, keepdims=False)
    mine = mine + send(mine, "yl", 1)
    return mine, send(mine, "c", 1)


def split(value):
    high = value.astype(jnp.bfloat16)
    low = (value - high.astype(jnp.float32)).astype(jnp.bfloat16)
    return high, low


def put_operand(real, imag, high_ref, low_ref):
    depth, width = real.shape
    for ref, re, im in zip((high_ref, low_ref), split(real), split(imag)):
        ref[:depth, :width] = re
        ref[:depth, width:] = im
        ref[depth:, :width] = -im
        ref[depth:, width:] = re


def product(real, imag, high_ref, low_ref):
    dot = functools.partial(jnp.dot, preferred_element_type=jnp.float32)
    (re_high, re_low), (im_high, im_low) = split(real), split(imag)
    high = cat([re_high, im_high], axis=1)
    low = cat([re_low, im_low], axis=1)
    return dot(low, high_ref[...]) + dot(high, low_ref[...]) + dot(high, high_ref[...])


def solve_kernel(src_ref, pos_ref, own_ref, peer_ref, mine_ref, other_ref, out_ref, inv_ref, high_ref, low_ref):
    core = pos_ref[0]
    width = mine_ref.shape[1]

    @pl.loop(0, 64)
    def _(j):
        row = pl.multiple_of(src_ref[j] * 8, 8)
        inv_ref[core, pl.ds(row, 8), :] = own_ref[j]
        inv_ref[1 - core, pl.ds(row, 8), :] = peer_ref[j]

    first = core == 0
    mine, other = mine_ref[...], other_ref[...]
    put_operand(jnp.where(first, mine, other), jnp.where(first, other, mine), high_ref, low_ref)

    @pl.loop(0, 2)
    def _(m):
        rows = pl.ds(pl.multiple_of(m * 256, 256), 256)
        both = product(inv_ref[0, rows, :], inv_ref[1, rows, :], high_ref, low_ref)
        out_ref[0, rows, :] = both[:, :width]
        out_ref[1, rows, :] = both[:, width:]


def solve(sources_b, position, own, peer, node, mine, other):
    whole = pl.BlockSpec(mine.shape, lambda i, *_: (0, 0))
    piece = pl.BlockSpec((64, 8, 512), lambda i, *_: (0, node, 0))
    depth, width = mine.shape
    return pl.pallas_call(
        solve_kernel,
        grid_spec=pltpu.PrefetchScalarGridSpec(
            num_scalar_prefetch=2,
            grid=(1,),
            in_specs=[piece, piece, whole, whole],
            out_specs=pl.BlockSpec((2, depth, width), lambda i, *_: (0, 0, 0)),
            scratch_shapes=[
                pltpu.VMEM((2, depth, depth), jnp.float32),
                pltpu.VMEM((2 * depth, 2 * width), jnp.bfloat16),
                pltpu.VMEM((2 * depth, 2 * width), jnp.bfloat16),
            ],
        ),
        out_shape=jax.ShapeDtypeStruct((2, depth, width), jnp.float32),
        cost_estimate=pl.CostEstimate(flops=6 * 2 * depth * 2 * depth * 2 * width, bytes_accessed=6 * MIB, transcendentals=0),
        compiler_params=pltpu.CompilerParams(vmem_limit_bytes=32 * MIB),
        name="solve",
    )(sources_b, position, own, peer, mine, other)


def update_kernel(pieces, next_pivot, src_ref, slot_ref, pos_ref, *refs):
    panel_refs = refs[:pieces]
    solved_ref, front_ref = refs[pieces : pieces + 2]
    outs = refs[pieces + 2 : -3]
    out_ref = outs[0]
    update_ref, high_ref, low_ref = refs[-3:]
    width = solved_ref.shape[2]
    depth = solved_ref.shape[1]
    put_operand(solved_ref[0], solved_ref[1], high_ref, low_ref)
    out_ref[...] = front_ref[...]

    @pl.when(pos_ref[0] == 1)
    def _():
        out_ref[:, pl.ds(pl.multiple_of(pos_ref[1], 512), depth), :] = solved_ref[...]

    done = 0
    for ref in panel_refs:
        count = ref.shape[0]
        step = min(count, 8)

        @pl.loop(0, count // step)
        def _(m, ref=ref, step=step, done=done):
            part = ref[pl.ds(m * step, step)]
            real = part[:, :16, :].reshape(step * 16, 512)
            imag = part[:, 16:, :].reshape(step * 16, 512)
            rows = pl.ds(pl.multiple_of(done * 16 + m * (step * 16), 64), step * 16)
            update_ref[rows, :] = product(real, imag, high_ref, low_ref)

        done += count

    def row_step(i, target):
        u = update_ref[pl.ds(i, 1), :]
        for part in range(2):
            out_ref[part, pl.ds(target, 1), :] = (
                out_ref[part, pl.ds(target, 1), :] - u[:, part * width : (part + 1) * width]
            )

    @pl.loop(0, 128)
    def _(g):
        base = src_ref[g // 2] * 16 + (g % 2) * 8
        targets = [slot_ref[base + i] for i in range(8)]

        @pl.when(targets[7] >= 0)
        def _():
            new = []
            for i in range(8):
                u = update_ref[pl.ds(g * 8 + i, 1), :]
                for part in range(2):
                    new.append(
                        out_ref[part, pl.ds(targets[i], 1), :] - u[:, part * width : (part + 1) * width]
                    )
            for i in range(8):
                for part in range(2):
                    out_ref[part, pl.ds(targets[i], 1), :] = new[2 * i + part]

        @pl.when((targets[7] < 0) & (targets[0] >= 0))
        def _():
            for i in range(8):

                @pl.when(targets[i] >= 0)
                def _(i=i):
                    row_step(g * 8 + i, targets[i])

    if next_pivot:
        rows = out_ref[:, pl.ds(pl.multiple_of(pos_ref[3], 512), depth), :]
        outs[1][...] = jnp.where(pos_ref[2] == 1, rows, 0.0)


def update(sources, slots, position, panels, solved, front, next_pivot):
    _, depth, width = solved.shape
    whole = lambda a: pl.BlockSpec(a.shape, lambda i, *_, n=a.ndim: (0,) * n, pipeline_mode=pl.Buffered(1))
    shapes = [jax.ShapeDtypeStruct(front.shape, jnp.float32)]
    if next_pivot:
        shapes.append(jax.ShapeDtypeStruct(solved.shape, jnp.float32))
    return pl.pallas_call(
        functools.partial(update_kernel, len(panels), next_pivot),
        grid_spec=pltpu.PrefetchScalarGridSpec(
            num_scalar_prefetch=3,
            grid=(1,),
            in_specs=[whole(a) for a in panels] + [whole(solved), whole(front)],
            out_specs=[whole(s) for s in shapes],
            scratch_shapes=[
                pltpu.VMEM((1024, 2 * width), jnp.float32),
                pltpu.VMEM((2 * depth, 2 * width), jnp.bfloat16),
                pltpu.VMEM((2 * depth, 2 * width), jnp.bfloat16),
            ],
        ),
        out_shape=shapes,
        cost_estimate=pl.CostEstimate(flops=6 * 2 * 1024 * depth * 2 * width, bytes_accessed=13 * MIB, transcendentals=0),
        compiler_params=pltpu.CompilerParams(vmem_limit_bytes=40 * MIB),
        name="update",
    )(sources, slots, position, *panels, solved, front)


def local(right_side, pivot_inverse, ancestor_panel, ancestors, pivot_block):
    depth = pivot_inverse.shape[3]
    per_device = right_side.shape[1] // depth
    core = lax.axis_index("c")
    row_index = lax.axis_index("yl") * 2 + core
    owned = (pivot_block // per_device == row_index).astype(jnp.int32)
    offset = (pivot_block % per_device * depth).astype(jnp.int32)
    position = jnp.stack([owned[0], offset[0], owned[1], offset[1]])
    position_last = jnp.stack([owned[1], offset[1]])
    core_position = core.astype(jnp.int32)[None]
    sources_a, sources_b = sources(offsets_a()), sources(offsets_b())

    inverse = lax.dynamic_index_in_dim(pivot_inverse, core, 1, keepdims=False).reshape(1, 16, depth)
    panel0 = ancestor_panel[0].reshape(1, 32, depth)
    panel1 = ancestor_panel[1].reshape(1, 32, depth)

    pair_a = cat([panel0, send(panel0, "yh", 1)])
    own_b = cat([inverse, panel1], axis=1)
    pair_b = cat([own_b, send(own_b, "yh", 1)])

    pivot0 = lax.dynamic_slice_in_dim(right_side, offset[0], depth, 1)
    mine0, other0 = from_owner(jnp.where(owned[0] == 1, pivot0, 0.0))

    block_a = cat([pair_a, send(pair_a, "x", 1), send(pair_a, "x", -1), send(pair_a, "x", 2)])
    blocks_b = ring_z_short(pair_b)
    blocks_a = ring_z(block_a)
    inverse_b = cat([v[:, :16] for v in blocks_b])
    panel_b = cat([v[:, 16:] for v in blocks_b])
    inverses = cat(ring_x(inverse_b))
    peer_inverses = send(inverses, "c", 1)
    blocks_b = ring_x(panel_b)

    solved0 = solve(sources_b, core_position, inverses, peer_inverses, 0, mine0, other0)
    front, pivot1 = update(sources_a, ancestors[0], position, blocks_a, solved0, right_side, True)
    mine1, other1 = from_owner(pivot1)
    solved1 = solve(sources_b, core_position, inverses, peer_inverses, 1, mine1, other1)
    (front,) = update(sources_b, ancestors[1], position_last, blocks_b, solved1, front, False)
    return front


def solution(mesh):
    torus = Mesh(mesh.devices.reshape(tuple(SIZES.values())), tuple(SIZES))
    in_specs = (
        P(None, ROW, SRC),
        P(None, None, SRC, None),
        P(None, None, ROW + SRC, None),
        P(None, ROW),
        P(),
    )
    return jax.shard_map(local, mesh=torus, in_specs=in_specs, out_specs=P(None, ROW, SRC), check_vma=False)
```

```python
import functools

import jax
import jax.numpy as jnp
import numpy as np
from jax import lax
from jax.experimental import pallas as pl
from jax.experimental.pallas import tpu as pltpu
from jax.sharding import Mesh, PartitionSpec as P


SIZES = {"yh": 2, "z": 8, "x": 4, "yl": 2, "c": 2}
SRC = ("yh", "z", "x")
ROW = ("yl", "c")
MIB = 1024 * 1024
cat = jnp.concatenate


def send(value, axis, shift):
    size = SIZES[axis]
    return lax.ppermute(value, axis, [(i, (i + shift) % size) for i in range(size)])


def ring_z(own):
    half = own.shape[0] // 2
    go = lambda value, shift: send(value, "z", shift)
    up1, down1 = go(own, 1), go(own, -1)
    up2, down2 = go(up1, 1), go(down1, -1)
    up3, down3 = go(up2, 1), go(down2, -1)
    up4, down4 = go(up3[:half], 1), go(down3[half:], -1)
    return [own, up1, down1, up2, down2, up3, down3, up4, down4]


def ring_z_short(own):
    half = own.shape[0] // 2
    go = lambda value, shift: send(value, "z", shift)
    up1, down1 = go(own, 1), go(own, -1)
    up2, down2 = go(own, 2), go(own, -2)
    up3, down3 = go(up2, 1), go(down2, -1)
    up4, down4 = go(up2[:half], 2), go(down2[half:], -2)
    return [own, up1, down1, up2, down2, up3, down3, up4, down4]


def ring_x(own):
    half = own.shape[0] // 2
    go = lambda value, shift: send(value, "x", shift)
    up1, down1 = go(own, 1), go(own, -1)
    up2, down2 = go(up1[:half], 1), go(down1[half:], -1)
    return [own, up1, down1, up2, down2]


Z_STEPS = [0, -1, 1, -2, 2, -3, 3]
X_STEPS = [0, -1, 1]


def offsets_a():
    block = [(dy, dx) for dx in (0, -1, 1, -2) for dy in (0, 1)]
    rows = [(dy, dz, dx) for dz in Z_STEPS for dy, dx in block]
    rows += [(dy, 4, dx) for dy, dx in block]
    return np.array(rows, np.int32)


def offsets_b():
    block = [(dy, dz) for dz in Z_STEPS + [4] for dy in (0, 1)]
    rows = [(dy, dz, dx) for dx in X_STEPS + [2] for dy, dz in block]
    return np.array(rows, np.int32)


def sources(offsets):
    yh, z, x = (lax.axis_index(a) for a in SRC)
    return (
        ((yh + offsets[:, 0]) % 2) * 32 + ((z + offsets[:, 1]) % 8) * 4 + (x + offsets[:, 2]) % 4
    ).astype(jnp.int32)


def from_owner(mine, other):
    mine = mine + send(other, "c", 1)
    mine = mine + send(mine, "yl", 1)
    return mine, send(mine, "c", 1)


def pack_kernel(rows, pieces, *refs):
    outs = refs[pieces:]
    done = 0
    for ref in refs[:pieces]:
        count = ref.shape[0]
        first = 0
        for out, height in zip(outs, rows):
            out[done : done + count] = ref[:, first : first + height, :]
            first += height
        done += count


def pack(pieces, rows):
    count, depth = sum(p.shape[0] for p in pieces), pieces[0].shape[2]
    whole = lambda a: pl.BlockSpec(a.shape, lambda: (0,) * 3)
    shapes = [jax.ShapeDtypeStruct((count, height, depth), jnp.float32) for height in rows]
    return pl.pallas_call(
        functools.partial(pack_kernel, rows, len(pieces)),
        in_specs=[whole(p) for p in pieces],
        out_specs=[whole(s) for s in shapes],
        out_shape=shapes,
        cost_estimate=pl.CostEstimate(flops=0, bytes_accessed=3 * MIB, transcendentals=0),
        compiler_params=pltpu.CompilerParams(vmem_limit_bytes=8 * MIB),
        name="pack",
    )(*pieces)


def order_kernel(src_ref, *refs):
    pieces, outs = refs[:-2], refs[-2:]
    done = 0
    for ref in pieces:

        @pl.loop(0, ref.shape[0])
        def _(j, ref=ref, done=done):
            row = pl.multiple_of(src_ref[done + j] * 8, 8)
            for node, out in enumerate(outs):
                out[pl.ds(row, 8), :] = ref[j, node * 8 : node * 8 + 8, :]

        done += ref.shape[0]


def order(sources, pieces):
    depth = pieces[0].shape[2]
    whole = lambda a: pl.BlockSpec(a.shape, lambda i, *_, n=len(a.shape): (0,) * n, pipeline_mode=pl.Buffered(1))
    shapes = [jax.ShapeDtypeStruct((depth, depth), jnp.float32)] * 2
    return pl.pallas_call(
        order_kernel,
        grid_spec=pltpu.PrefetchScalarGridSpec(
            num_scalar_prefetch=1,
            grid=(1,),
            in_specs=[whole(p) for p in pieces],
            out_specs=[whole(s) for s in shapes],
        ),
        out_shape=shapes,
        cost_estimate=pl.CostEstimate(flops=0, bytes_accessed=4 * MIB, transcendentals=0),
        compiler_params=pltpu.CompilerParams(vmem_limit_bytes=8 * MIB),
        name="order",
    )(sources, *pieces)


def split(value):
    high = value.astype(jnp.bfloat16)
    low = (value - high.astype(jnp.float32)).astype(jnp.bfloat16)
    return high, low


def put_operand(real, imag, high_ref, low_ref):
    depth, width = real.shape
    for ref, re, im in zip((high_ref, low_ref), split(real), split(imag)):
        ref[:depth, :width] = re
        ref[:depth, width:] = im
        ref[depth:, :width] = -im
        ref[depth:, width:] = re


def product(real, imag, high_ref, low_ref):
    dot = functools.partial(jnp.dot, preferred_element_type=jnp.float32)
    (re_high, re_low), (im_high, im_low) = split(real), split(imag)
    high = cat([re_high, im_high], axis=1)
    low = cat([re_low, im_low], axis=1)
    return dot(low, high_ref[...]) + dot(high, low_ref[...]) + dot(high, high_ref[...])


def solve_into(core, own_ref, peer_ref, mine_ref, other_ref, out_ref, high_ref, low_ref):
    width = mine_ref.shape[1]
    first = core == 0
    mine, other = mine_ref[...], other_ref[...]
    put_operand(jnp.where(first, mine, other), jnp.where(first, other, mine), high_ref, low_ref)

    @pl.loop(0, 2)
    def _(m):
        rows = pl.ds(pl.multiple_of(m * 256, 256), 256)
        own, peer = own_ref[rows, :], peer_ref[rows, :]
        both = product(jnp.where(first, own, peer), jnp.where(first, peer, own), high_ref, low_ref)
        out_ref[0, rows, :] = both[:, :width]
        out_ref[1, rows, :] = both[:, width:]


def solve_kernel(pos_ref, *refs):
    solve_into(pos_ref[0], *refs)


def solve(position, own, peer, mine, other):
    whole = lambda a: pl.BlockSpec(a.shape, lambda i, *_: (0, 0))
    depth, width = mine.shape
    return pl.pallas_call(
        solve_kernel,
        grid_spec=pltpu.PrefetchScalarGridSpec(
            num_scalar_prefetch=1,
            grid=(1,),
            in_specs=[whole(own), whole(peer), whole(mine), whole(other)],
            out_specs=pl.BlockSpec((2, depth, width), lambda i, *_: (0, 0, 0)),
            scratch_shapes=[
                pltpu.VMEM((2 * depth, 2 * width), jnp.bfloat16),
                pltpu.VMEM((2 * depth, 2 * width), jnp.bfloat16),
            ],
        ),
        out_shape=jax.ShapeDtypeStruct((2, depth, width), jnp.float32),
        cost_estimate=pl.CostEstimate(flops=6 * 2 * depth * 2 * depth * 2 * width, bytes_accessed=6 * MIB, transcendentals=0),
        compiler_params=pltpu.CompilerParams(vmem_limit_bytes=24 * MIB),
        name="solve",
    )(position, own, peer, mine, other)


def multiply_panel(part, high_ref, low_ref):
    count, depth = part.shape[0], part.shape[2]
    real = part[:, :16, :].reshape(count * 16, depth)
    imag = part[:, 16:, :].reshape(count * 16, depth)
    return product(real, imag, high_ref, low_ref)


def project_kernel(pieces, first, src_ref, pos_ref, *refs):
    panel_refs = refs[:pieces]
    high_ref, low_ref = refs[-2:]
    if first:
        solved_ref, out_ref = refs[pieces : pieces + 2]
        done = 0
    else:
        solved_ref, so_far_ref, pivot_ref, out_ref, mine_ref, other_ref, sums_ref = refs[pieces:-2]
        done = 64 - sum(r.shape[0] for r in panel_refs)
        sums_ref[:1024, :] = so_far_ref[...]
    target_ref = out_ref if first else sums_ref
    put_operand(solved_ref[0], solved_ref[1], high_ref, low_ref)
    for ref in panel_refs:
        count = ref.shape[0]
        result = multiply_panel(ref[...], high_ref, low_ref)
        for j in range(count):
            row = pl.multiple_of(src_ref[done + j] * 16, 16)
            target_ref[pl.ds(row, 16), :] = result[j * 16 : (j + 1) * 16]
        done += count
    if not first:
        out_ref[...] = sums_ref[:1024, :]
        depth, width = mine_ref.shape

        @pl.when(pos_ref[2] == 1)
        def _():
            start = pos_ref[5]
            past = start % 8
            turn = (8 - past) % 8
            in_first = lax.broadcasted_iota(jnp.int32, (8, 2 * width), 0) < 8 - past
            core_first = pos_ref[4] == 0

            @pl.loop(0, depth // 8)
            def _(m):
                rows = pl.ds(pl.multiple_of(m * 8, 8), 8)
                base = pl.multiple_of(start - past + m * 8, 8)
                upper = pltpu.roll(sums_ref[pl.ds(base, 8), :], turn, 0)
                lower = pltpu.roll(sums_ref[pl.ds(base + 8, 8), :], turn, 0)
                taken = jnp.where(in_first, upper, lower)
                real = pivot_ref[0, rows, :] - taken[:, :width]
                imag = pivot_ref[1, rows, :] - taken[:, width:]
                mine_ref[rows, :] = jnp.where(core_first, real, imag)
                other_ref[rows, :] = jnp.where(core_first, imag, real)

        @pl.when(pos_ref[2] == 0)
        def _():
            mine_ref[...] = jnp.zeros_like(mine_ref)
            other_ref[...] = jnp.zeros_like(other_ref)


def whole(array):
    return pl.BlockSpec(array.shape, lambda i, *_, n=len(array.shape): (0,) * n, pipeline_mode=pl.Buffered(1))


def project(sources, position, panels, solved, so_far=None, pivot=None):
    _, depth, width = solved.shape
    first = so_far is None
    inputs = [*panels, solved] + ([] if first else [so_far, pivot])
    shapes = [jax.ShapeDtypeStruct((1024, 2 * width), jnp.float32)]
    scratch = [pltpu.VMEM((2 * depth, 2 * width), jnp.bfloat16)] * 2
    if not first:
        shapes += [jax.ShapeDtypeStruct((depth, width), jnp.float32)] * 2
        scratch = [pltpu.VMEM((1032, 2 * width), jnp.float32)] + scratch
    return pl.pallas_call(
        functools.partial(project_kernel, len(panels), first),
        grid_spec=pltpu.PrefetchScalarGridSpec(
            num_scalar_prefetch=2,
            grid=(1,),
            in_specs=[whole(a) for a in inputs],
            out_specs=[whole(s) for s in shapes],
            scratch_shapes=scratch,
        ),
        out_shape=shapes,
        cost_estimate=pl.CostEstimate(flops=3 * 2 * 1024 * depth * 2 * width, bytes_accessed=6 * MIB, transcendentals=0),
        compiler_params=pltpu.CompilerParams(vmem_limit_bytes=24 * MIB),
        name="project",
    )(sources, position, *inputs)


def subtract_rows(front_ref, update_ref, first, targets):
    width = front_ref.shape[2]
    new = []
    for i, target in enumerate(targets):
        row = update_ref[pl.ds(first + i, 1), :]
        for part in range(2):
            new.append(front_ref[part, pl.ds(target, 1), :] - row[:, part * width : (part + 1) * width])
    for i, target in enumerate(targets):
        for part in range(2):
            front_ref[part, pl.ds(target, 1), :] = new[2 * i + part]


def slot_targets(slot_ref, base, count, rows):
    slots = [slot_ref[base + i] for i in range(count)]
    return [jnp.where(slot >= 0, slot, rows + i % 8) for i, slot in enumerate(slots)]


def load_front(front_ref, held_ref, sem):
    rows = front_ref.shape[1]
    return [
        pltpu.make_async_copy(front_ref.at[part], held_ref.at[part, pl.ds(0, rows), :], sem.at[part])
        for part in range(2)
    ]


def store_front(held_ref, out_ref, sem):
    rows = out_ref.shape[1]
    return [
        pltpu.make_async_copy(held_ref.at[part, pl.ds(0, rows), :], out_ref.at[part], sem.at[part])
        for part in range(2)
    ]


def scatter_kernel(slot_ref, pos_ref, front_ref, update_ref, solved_ref, out_ref, held_ref, sem):
    rows, depth = front_ref.shape[1], solved_ref.shape[1]
    copies = load_front(front_ref, held_ref, sem)
    for copy in copies:
        copy.start()
    for copy in copies:
        copy.wait()

    @pl.when(pos_ref[0] == 1)
    def _():
        held_ref[:, pl.ds(pl.multiple_of(pos_ref[1], 512), depth), :] = solved_ref[...]

    @pl.loop(0, 64)
    def _(g):
        subtract_rows(held_ref, update_ref, g * 16, slot_targets(slot_ref, g * 16, 16, rows))

    copies = store_front(held_ref, out_ref, sem)
    for copy in copies:
        copy.start()
    for copy in copies:
        copy.wait()


def scatter(slots, position, front, update, solved):
    anywhere = pl.BlockSpec(memory_space=pl.ANY)
    _, rows, width = front.shape
    return pl.pallas_call(
        scatter_kernel,
        grid_spec=pltpu.PrefetchScalarGridSpec(
            num_scalar_prefetch=2,
            grid=(1,),
            in_specs=[anywhere, whole(update), whole(solved)],
            out_specs=anywhere,
            scratch_shapes=[pltpu.VMEM((2, rows + 8, width), jnp.float32), pltpu.SemaphoreType.DMA((2,))],
        ),
        out_shape=jax.ShapeDtypeStruct(front.shape, jnp.float32),
        cost_estimate=pl.CostEstimate(flops=MIB, bytes_accessed=24 * MIB, transcendentals=0),
        compiler_params=pltpu.CompilerParams(vmem_limit_bytes=24 * MIB),
        name="scatter",
    )(slots, position, front, update, solved)


def finish_kernel(pieces, src_ref, slot_ref, pos_ref, *refs):
    panel_refs = refs[:pieces]
    own_ref, peer_ref, mine_ref, other_ref, front_ref, out_ref = refs[pieces : pieces + 6]
    held_ref, solved_ref, update_ref, high_ref, low_ref, sem = refs[pieces + 6 :]
    rows = front_ref.shape[1]
    depth, _ = mine_ref.shape
    copies = load_front(front_ref, held_ref, sem)
    for copy in copies:
        copy.start()
    solve_into(pos_ref[4], own_ref, peer_ref, mine_ref, other_ref, solved_ref, high_ref, low_ref)
    put_operand(solved_ref[0], solved_ref[1], high_ref, low_ref)
    for copy in copies:
        copy.wait()

    @pl.when(pos_ref[2] == 1)
    def _():
        held_ref[:, pl.ds(pl.multiple_of(pos_ref[3], 512), depth), :] = solved_ref[...]

    chunks = [(ref, j) for ref in panel_refs for j in range(0, ref.shape[0], 8)]

    def put_down(m):
        for j in range(8):
            base = src_ref[m * 8 + j] * 16
            subtract_rows(held_ref, update_ref, m * 128 + j * 16, slot_targets(slot_ref, base, 16, rows))

    for m, (ref, j) in enumerate(chunks):
        update_ref[m * 128 : (m + 1) * 128, :] = multiply_panel(ref[j : j + 8], high_ref, low_ref)
        if m:
            put_down(m - 1)
    put_down(len(chunks) - 1)
    copies = store_front(held_ref, out_ref, sem)
    for copy in copies:
        copy.start()
    for copy in copies:
        copy.wait()


def finish(sources, slots, position, panels, own, peer, mine, other, front):
    anywhere = pl.BlockSpec(memory_space=pl.ANY)
    _, rows, width = front.shape
    depth = mine.shape[0]
    return pl.pallas_call(
        functools.partial(finish_kernel, len(panels)),
        grid_spec=pltpu.PrefetchScalarGridSpec(
            num_scalar_prefetch=3,
            grid=(1,),
            in_specs=[whole(a) for a in (*panels, own, peer, mine, other)] + [anywhere],
            out_specs=anywhere,
            scratch_shapes=[
                pltpu.VMEM((2, rows + 8, width), jnp.float32),
                pltpu.VMEM((2, depth, width), jnp.float32),
                pltpu.VMEM((1024, 2 * width), jnp.float32),
                pltpu.VMEM((2 * depth, 2 * width), jnp.bfloat16),
                pltpu.VMEM((2 * depth, 2 * width), jnp.bfloat16),
                pltpu.SemaphoreType.DMA((2,)),
            ],
        ),
        out_shape=jax.ShapeDtypeStruct(front.shape, jnp.float32),
        cost_estimate=pl.CostEstimate(flops=9 * 2 * 1024 * depth * 2 * width, bytes_accessed=13 * MIB, transcendentals=0),
        compiler_params=pltpu.CompilerParams(vmem_limit_bytes=32 * MIB),
        name="finish",
    )(sources, slots, position, *panels, own, peer, mine, other, front)


def program(right_side, pivot_inverse, ancestor_panel, ancestors, pivot_block):
    depth = pivot_inverse.shape[3]
    per_device = right_side.shape[1] // depth
    core = lax.axis_index("c")
    row_index = lax.axis_index("yl") * 2 + core
    owned = (pivot_block // per_device == row_index).astype(jnp.int32)
    offset = (pivot_block % per_device * depth).astype(jnp.int32)
    start = jnp.sum(((ancestors[0] >= 0) & (ancestors[0] < offset[1])).astype(jnp.int32))
    start = jnp.minimum(start, ancestors.shape[1] - depth)
    position = jnp.stack([owned[0], offset[0], owned[1], offset[1], core.astype(jnp.int32), start])
    core_position = core.astype(jnp.int32)[None]
    sources_a, sources_b = sources(offsets_a()), sources(offsets_b())

    inverse = lax.dynamic_index_in_dim(pivot_inverse, core, 1, keepdims=False).reshape(1, 16, depth)
    panel0 = ancestor_panel[0].reshape(1, 32, depth)
    panel1 = ancestor_panel[1].reshape(1, 32, depth)

    pair_a = cat([panel0, send(panel0, "yh", 1)])
    own_b = cat([inverse, panel1], axis=1)
    pair_b = cat([own_b, send(own_b, "yh", 1)])

    pivot0 = lax.dynamic_slice_in_dim(right_side, offset[0], depth, 1)
    pivot0 = jnp.where(owned[0] == 1, pivot0, 0.0)
    mine0, other0 = from_owner(
        lax.dynamic_index_in_dim(pivot0, core, 0, keepdims=False),
        lax.dynamic_index_in_dim(pivot0, 1 - core, 0, keepdims=False),
    )

    along_x = [pair_a, send(pair_a, "x", 1), send(pair_a, "x", -1), send(pair_a, "x", 2)]
    (block_a,) = pack(along_x, (32,))
    blocks_b = ring_z_short(pair_b)
    blocks_a = ring_z(block_a)
    inverse_b, panel_b = pack(blocks_b, (16, 32))
    inverse0, inverse1 = order(sources_b, ring_x(inverse_b))
    peer0 = send(inverse0, "c", 1)
    peer1 = send(inverse1, "c", 1)
    blocks_b = ring_x(panel_b)

    solved0 = solve(core_position, inverse0, peer0, mine0, other0)
    (early,) = project(sources_a, position, blocks_a[:5], solved0)
    pivot1 = lax.dynamic_slice_in_dim(right_side, offset[1], depth, 1)
    sums, mine1, other1 = project(sources_a, position, blocks_a[5:], solved0, early, pivot1)
    front = scatter(ancestors[0], position, right_side, sums, solved0)
    mine1, other1 = from_owner(mine1, other1)
    return finish(sources_b, ancestors[1], position, blocks_b, inverse1, peer1, mine1, other1, front)


def solution(mesh):
    torus = Mesh(mesh.devices.reshape(tuple(SIZES.values())), tuple(SIZES))
    in_specs = (
        P(None, ROW, SRC),
        P(None, None, SRC, None),
        P(None, None, ROW + SRC, None),
        P(None, ROW),
        P(),
    )
    return jax.shard_map(program, mesh=torus, in_specs=in_specs, out_specs=P(None, ROW, SRC), check_vma=False)
```

```python
import functools

import jax
import jax.numpy as jnp
from jax import lax
from jax.experimental import pallas as pl
from jax.experimental.pallas import tpu as pltpu
from jax.sharding import Mesh, PartitionSpec as P


SIZES = {"yh": 2, "z": 8, "x": 4, "yl": 2, "c": 2}
SRC = ("yh", "z", "x")
ROW = ("yl", "c")
MIB = 1024 * 1024
cat = jnp.concatenate


def send(value, axis, shift):
    size = SIZES[axis]
    return lax.ppermute(value, axis, [(i, (i + shift) % size) for i in range(size)])


def send_apart(value, axis, hops):
    size = SIZES[axis]
    pairs = [
        (i * 2 + core, (i + hops * (1 - 2 * core)) % size * 2 + core) for i in range(size) for core in range(2)
    ]
    return lax.ppermute(value, (axis, "c"), pairs)


def swap(value):
    return send(value, "c", 1)


def step_of(i):
    return ((i + 1) >> 1) * (1 - 2 * (i & 1))


def source(piece, x_outer):
    yh, z, x, sign = lax.axis_index("yh"), lax.axis_index("z"), lax.axis_index("x"), 1 - 2 * lax.axis_index("c")
    if x_outer:
        dx, dz = step_of(piece >> 4) * sign, step_of((piece >> 1) & 7)
    else:
        dz, dx = step_of(piece >> 3) * sign, step_of((piece >> 1) & 3)
    return ((yh + piece) & 1) * 32 + ((z + dz) & 7) * 4 + ((x + dx) & 3)


def owner_of(block):
    row = lax.axis_index("yl") * 2 + lax.axis_index("c")
    return block >> 2 == row, pl.multiple_of((block & 3) * 512, 512)


def prepare_kernel(inverse_ref, panel_ref, panel0_ref, own_b_ref):
    core = lax.axis_index("c")
    for node in range(2):
        own_b_ref[0, node * 8 : node * 8 + 8, :] = inverse_ref[node, core]
    for part in range(2):
        panel0_ref[0, part * 16 : part * 16 + 16, :] = panel_ref[0, part]
        own_b_ref[0, 16 + part * 16 : 32 + part * 16, :] = panel_ref[1, part]


def prepare(inverse, panel):
    depth = panel.shape[3]
    return pl.pallas_call(
        prepare_kernel,
        out_shape=[jax.ShapeDtypeStruct((1, rows, depth), jnp.float32) for rows in (32, 48)],
        compiler_params=pltpu.CompilerParams(vmem_limit_bytes=4 * MIB),
        name="prepare",
    )(inverse, panel)


def take_kernel(block_ref, front_ref, mine_ref, other_ref, rows_ref, sem):
    owned, first = owner_of(block_ref[0])
    core = lax.axis_index("c")

    @pl.when(owned)
    def _():
        copy = pltpu.make_async_copy(front_ref.at[:, pl.ds(first, rows_ref.shape[1]), :], rows_ref, sem)
        copy.start()
        copy.wait()
        mine_ref[...] = rows_ref[core]
        other_ref[...] = rows_ref[1 - core]

    @pl.when(jnp.logical_not(owned))
    def _():
        mine_ref[...] = jnp.zeros_like(mine_ref)
        other_ref[...] = jnp.zeros_like(other_ref)


def take(blocks, front, depth):
    width = front.shape[2]
    shapes = [jax.ShapeDtypeStruct((depth, width), jnp.float32)] * 2
    return pl.pallas_call(
        take_kernel,
        grid_spec=pltpu.PrefetchScalarGridSpec(
            num_scalar_prefetch=1,
            grid=(1,),
            in_specs=[ANYWHERE],
            out_specs=[whole(s) for s in shapes],
            scratch_shapes=[pltpu.VMEM((2, depth, width), jnp.float32), pltpu.SemaphoreType.DMA],
        ),
        out_shape=shapes,
        cost_estimate=pl.CostEstimate(flops=0, bytes_accessed=2 * MIB, transcendentals=0),
        compiler_params=pltpu.CompilerParams(vmem_limit_bytes=8 * MIB),
        name="take",
    )(blocks, front)


def from_owner(mine, other):
    mine = mine + swap(other)
    mine = mine + send(mine, "yl", 1)
    return mine, swap(mine)


def pack_kernel(rows, own_ref, *refs):
    pairs, outs = refs[: -2 * len(rows)], refs[-2 * len(rows) :]
    core = lax.axis_index("c")
    steps = len(pairs) // 2
    first = 0
    for which, height in enumerate(rows):
        part = slice(first, first + height)
        for who in range(2):
            out = outs[2 * which + who]
            out[0] = own_ref[who * 2 : who * 2 + 2, part, :]
            for k in range(1, steps):
                near, far = pairs[2 * k - 2 : 2 * k]
                out[2 * k - 1 + core] = near[who * 2 : who * 2 + 2, part, :]
                out[2 * k - core] = far[2 - who * 2 : 4 - who * 2, part, :]
            out[2 * steps - 1] = pairs[2 * steps - 2 + who][:, part, :]
        first += height


def pack(own, pairs, rows):
    steps, depth = len(pairs), own.shape[2]
    shapes = [jax.ShapeDtypeStruct((steps, 2, h, depth), jnp.float32) for h in rows for _ in range(2)]
    outs = pl.pallas_call(
        functools.partial(pack_kernel, rows),
        grid=(1,),
        in_specs=[whole(a) for a in (own, *pairs)],
        out_specs=[whole(s) for s in shapes],
        out_shape=shapes,
        cost_estimate=pl.CostEstimate(flops=0, bytes_accessed=3 * MIB, transcendentals=0),
        compiler_params=pltpu.CompilerParams(vmem_limit_bytes=12 * MIB),
        name="pack",
    )(own, *pairs)
    return [out.reshape(steps * 2, *out.shape[2:]) for out in outs]


def whole(array):
    return pl.BlockSpec(array.shape, lambda i, *_, n=len(array.shape): (0,) * n, pipeline_mode=pl.Buffered(1))


ANYWHERE = pl.BlockSpec(memory_space=pl.ANY)


def order_kernel(*refs):
    pieces, outs = refs[:-2], refs[-2:]
    done = 0
    for own, other in zip(pieces[::2], pieces[1::2]):
        count = own.shape[0]

        @pl.loop(0, count)
        def _(j, own=own, other=other, done=done):
            row = pl.multiple_of(source(done + j, True) * 8, 8)
            for node, out in enumerate(outs):
                out[0, pl.ds(row, 8), :] = own[j, node * 8 : node * 8 + 8, :]
                out[1, pl.ds(row, 8), :] = other[j, node * 8 : node * 8 + 8, :]

        done += count


def order(pieces):
    depth = pieces[0].shape[2]
    shapes = [jax.ShapeDtypeStruct((2, depth, depth), jnp.float32)] * 2
    return pl.pallas_call(
        order_kernel,
        grid=(1,),
        in_specs=[whole(a) for a in pieces],
        out_specs=[whole(s) for s in shapes],
        out_shape=shapes,
        cost_estimate=pl.CostEstimate(flops=0, bytes_accessed=8 * MIB, transcendentals=0),
        compiler_params=pltpu.CompilerParams(vmem_limit_bytes=12 * MIB),
        name="order",
    )(*pieces)


def split(value):
    high = value.astype(jnp.bfloat16)
    low = (value - high.astype(jnp.float32)).astype(jnp.bfloat16)
    return high, low


def put_operand(real, imag, high_ref, low_ref):
    depth, width = real.shape
    for ref, re, im in zip((high_ref, low_ref), split(real), split(imag)):
        ref[:depth, :width] = re
        ref[:depth, width:] = im
        ref[depth:, :width] = -im
        ref[depth:, width:] = re


def product(real, imag, high_ref, low_ref):
    dot = functools.partial(jnp.dot, preferred_element_type=jnp.float32)
    (re_high, re_low), (im_high, im_low) = split(real), split(imag)
    high = cat([re_high, im_high], axis=1)
    low = cat([re_low, im_low], axis=1)
    return dot(low, high_ref[...]) + dot(high, low_ref[...]) + dot(high, high_ref[...])


def solve_into(inverse_ref, mine_ref, other_ref, out_ref, high_ref, low_ref):
    width = mine_ref.shape[1]
    core = lax.axis_index("c")
    first = core == 0
    mine, other = mine_ref[...], other_ref[...]
    put_operand(jnp.where(first, mine, other), jnp.where(first, other, mine), high_ref, low_ref)

    @pl.loop(0, 2)
    def _(m):
        rows = pl.ds(pl.multiple_of(m * 256, 256), 256)
        both = product(inverse_ref[core, rows, :], inverse_ref[1 - core, rows, :], high_ref, low_ref)
        out_ref[0, rows, :] = both[:, :width]
        out_ref[1, rows, :] = both[:, width:]


def solve(inverse, mine, other):
    depth, width = mine.shape
    shape = jax.ShapeDtypeStruct((2, depth, width), jnp.float32)
    return pl.pallas_call(
        solve_into,
        grid=(1,),
        in_specs=[whole(inverse), whole(mine), whole(other)],
        out_specs=whole(shape),
        scratch_shapes=[pltpu.VMEM((2 * depth, 2 * width), jnp.bfloat16)] * 2,
        out_shape=shape,
        cost_estimate=pl.CostEstimate(flops=6 * 2 * depth * 2 * depth * 2 * width, bytes_accessed=6 * MIB, transcendentals=0),
        compiler_params=pltpu.CompilerParams(vmem_limit_bytes=24 * MIB),
        name="solve",
    )(inverse, mine, other)


def multiply_panel(part, high_ref, low_ref):
    count, depth = part.shape[0], part.shape[2]
    real = part[:, :16, :].reshape(count * 16, depth)
    imag = part[:, 16:, :].reshape(count * 16, depth)
    return product(real, imag, high_ref, low_ref)


def first_slot(slot_ref, row, last):
    low, high = jnp.int32(0), jnp.int32(last)
    for _ in range(10):
        middle = (low + high) >> 1
        slot = slot_ref[middle]
        before = (slot >= 0) & (slot < row)
        low, high = jnp.where(before, jnp.minimum(middle + 1, high), low), jnp.where(before, high, middle)
    return low


def load_pieces(refs, panel_ref, sem):
    copies, done = [], 0
    for i, ref in enumerate(refs):
        count = ref.shape[0]
        copies.append(pltpu.make_async_copy(ref, panel_ref.at[pl.ds(done, count)], sem.at[i]))
        done += count
    return copies


def project_kernel(pieces, done, first, block_ref, slot_ref, *refs):
    panel_refs = refs[:pieces]
    panel_ref, high_ref, low_ref, sem = refs[-4:]
    owned, first_row = owner_of(block_ref[1])
    copies = load_pieces(panel_refs, panel_ref, sem)
    for copy in copies:
        copy.start()
    if first:
        solved_ref, out_ref = refs[pieces : pieces + 2]
    else:
        solved_ref, so_far_ref, front_ref, out_ref, mine_ref, other_ref, sums_ref, pivot_ref, pivot_sem = refs[pieces:-4]
        depth, width = mine_ref.shape
        pivot = pltpu.make_async_copy(front_ref.at[:, pl.ds(first_row, depth), :], pivot_ref, pivot_sem)
        pivot.start()
        sums_ref[:1024, :] = so_far_ref[...]
    target_ref = out_ref if first else sums_ref
    put_operand(solved_ref[0], solved_ref[1], high_ref, low_ref)
    for copy in copies:
        copy.wait()

    @pl.loop(0, panel_ref.shape[0] // 8)
    def _(m):
        result = multiply_panel(panel_ref[pl.ds(m * 8, 8)], high_ref, low_ref)
        for j in range(8):
            row = pl.multiple_of(source(done + m * 8 + j, False) * 16, 16)
            target_ref[pl.ds(row, 16), :] = result[j * 16 : (j + 1) * 16]

    if not first:
        out_ref[...] = sums_ref[:1024, :]
        pivot.wait()

        @pl.when(owned)
        def _():
            start = first_slot(slot_ref, first_row, 1024 - depth)
            past = start & 7
            turn = (8 - past) & 7
            in_first = lax.broadcasted_iota(jnp.int32, (8, 2 * width), 0) < 8 - past
            core_first = lax.axis_index("c") == 0

            @pl.loop(0, depth // 8)
            def _(m):
                rows = pl.ds(pl.multiple_of(m * 8, 8), 8)
                base = pl.multiple_of(start - past + m * 8, 8)
                upper = pltpu.roll(sums_ref[pl.ds(base, 8), :], turn, 0)
                lower = pltpu.roll(sums_ref[pl.ds(base + 8, 8), :], turn, 0)
                taken = jnp.where(in_first, upper, lower)
                real = pivot_ref[0, rows, :] - taken[:, :width]
                imag = pivot_ref[1, rows, :] - taken[:, width:]
                mine_ref[rows, :] = jnp.where(core_first, real, imag)
                other_ref[rows, :] = jnp.where(core_first, imag, real)

        @pl.when(jnp.logical_not(owned))
        def _():
            mine_ref[...] = jnp.zeros_like(mine_ref)
            other_ref[...] = jnp.zeros_like(other_ref)


def project(blocks, slots, panels, done, solved, so_far=None, front=None):
    _, depth, width = solved.shape
    first = so_far is None
    inputs = [solved] if first else [solved, so_far]
    shapes = [jax.ShapeDtypeStruct((1024, 2 * width), jnp.float32)]
    in_specs = [ANYWHERE] * len(panels) + [whole(a) for a in inputs]
    scratch = [
        pltpu.VMEM((sum(a.shape[0] for a in panels), 32, depth), jnp.float32),
        pltpu.VMEM((2 * depth, 2 * width), jnp.bfloat16),
        pltpu.VMEM((2 * depth, 2 * width), jnp.bfloat16),
        pltpu.SemaphoreType.DMA((len(panels),)),
    ]
    if not first:
        inputs.append(front)
        in_specs.append(ANYWHERE)
        shapes += [jax.ShapeDtypeStruct((depth, width), jnp.float32)] * 2
        scratch = [
            pltpu.VMEM((1032, 2 * width), jnp.float32),
            pltpu.VMEM(solved.shape, jnp.float32),
            pltpu.SemaphoreType.DMA,
        ] + scratch
    return pl.pallas_call(
        functools.partial(project_kernel, len(panels), done, first),
        grid_spec=pltpu.PrefetchScalarGridSpec(
            num_scalar_prefetch=2,
            grid=(1,),
            in_specs=in_specs,
            out_specs=[whole(s) for s in shapes],
            scratch_shapes=scratch,
        ),
        out_shape=shapes,
        cost_estimate=pl.CostEstimate(flops=3 * 2 * 1024 * depth * 2 * width, bytes_accessed=6 * MIB, transcendentals=0),
        compiler_params=pltpu.CompilerParams(vmem_limit_bytes=24 * MIB),
        name="project",
    )(blocks, slots, *panels, *inputs)


def subtract_rows(front_ref, update_ref, first, targets):
    width = front_ref.shape[2]
    new = []
    for i, target in enumerate(targets):
        row = update_ref[pl.ds(first + i, 1), :]
        for part in range(2):
            new.append(front_ref[part, pl.ds(target, 1), :] - row[:, part * width : (part + 1) * width])
    for i, target in enumerate(targets):
        for part in range(2):
            front_ref[part, pl.ds(target, 1), :] = new[2 * i + part]


def slot_targets(slot_ref, base, count, rows):
    slots = [slot_ref[base + i] for i in range(count)]
    return [jnp.where(slot >= 0, slot, rows + i % 8) for i, slot in enumerate(slots)]


def load_front(front_ref, held_ref, sem):
    rows = front_ref.shape[1]
    return [
        pltpu.make_async_copy(front_ref.at[part], held_ref.at[part, pl.ds(0, rows), :], sem.at[part])
        for part in range(2)
    ]


def store_front(held_ref, out_ref, sem):
    rows = out_ref.shape[1]
    return [
        pltpu.make_async_copy(held_ref.at[part, pl.ds(0, rows), :], out_ref.at[part], sem.at[part])
        for part in range(2)
    ]


def scatter_kernel(block_ref, slot_ref, front_ref, update_ref, solved_ref, out_ref, held_ref, sem):
    rows, depth = front_ref.shape[1], solved_ref.shape[1]
    copies = load_front(front_ref, held_ref, sem)
    for copy in copies:
        copy.start()
    for copy in copies:
        copy.wait()

    owned, first_row = owner_of(block_ref[0])

    @pl.when(owned)
    def _():
        held_ref[:, pl.ds(first_row, depth), :] = solved_ref[...]

    @pl.loop(0, 64)
    def _(g):
        subtract_rows(held_ref, update_ref, g * 16, slot_targets(slot_ref, g * 16, 16, rows))

    copies = store_front(held_ref, out_ref, sem)
    for copy in copies:
        copy.start()
    for copy in copies:
        copy.wait()


def scatter(blocks, slots, front, update, solved):
    _, rows, width = front.shape
    return pl.pallas_call(
        scatter_kernel,
        grid_spec=pltpu.PrefetchScalarGridSpec(
            num_scalar_prefetch=2,
            grid=(1,),
            in_specs=[ANYWHERE, whole(update), whole(solved)],
            out_specs=ANYWHERE,
            scratch_shapes=[pltpu.VMEM((2, rows + 8, width), jnp.float32), pltpu.SemaphoreType.DMA((2,))],
        ),
        out_shape=jax.ShapeDtypeStruct(front.shape, jnp.float32),
        cost_estimate=pl.CostEstimate(flops=MIB, bytes_accessed=24 * MIB, transcendentals=0),
        compiler_params=pltpu.CompilerParams(vmem_limit_bytes=24 * MIB),
        name="scatter",
    )(blocks, slots, front, update, solved)


def finish_kernel(pieces, block_ref, slot_ref, *refs):
    inverse_ref, mine_ref, other_ref, front_ref, out_ref = refs[pieces : pieces + 5]
    held_ref, solved_ref, panel_ref, even_ref, odd_ref, high_ref, low_ref, front_sem, sem = refs[pieces + 5 :]
    rows = front_ref.shape[1]
    depth, _ = mine_ref.shape
    copies = load_pieces(refs[:pieces], panel_ref, sem) + load_front(front_ref, held_ref, front_sem)
    for copy in copies:
        copy.start()
    solve_into(inverse_ref, mine_ref, other_ref, solved_ref, high_ref, low_ref)
    put_operand(solved_ref[0], solved_ref[1], high_ref, low_ref)
    for copy in copies:
        copy.wait()

    owned, first_row = owner_of(block_ref[1])

    @pl.when(owned)
    def _():
        held_ref[:, pl.ds(first_row, depth), :] = solved_ref[...]

    def put_down(update_ref, m, skip=None):
        for j in range(8):
            base = source(jnp.maximum(m * 8 + j, 0), True) * 16
            targets = slot_targets(slot_ref, base, 16, rows)
            if skip is not None:
                targets = [jnp.where(skip, rows + i % 8, t) for i, t in enumerate(targets)]
            subtract_rows(held_ref, update_ref, j * 16, targets)

    @pl.loop(0, 4)
    def _(m):
        even_ref[...] = multiply_panel(panel_ref[pl.ds(m * 16, 8)], high_ref, low_ref)
        put_down(odd_ref, 2 * m - 1, skip=m == 0)
        odd_ref[...] = multiply_panel(panel_ref[pl.ds(m * 16 + 8, 8)], high_ref, low_ref)
        put_down(even_ref, 2 * m)

    put_down(odd_ref, 7)
    copies = store_front(held_ref, out_ref, front_sem)
    for copy in copies:
        copy.start()
    for copy in copies:
        copy.wait()


def finish(blocks, slots, panels, inverse, mine, other, front):
    _, rows, width = front.shape
    depth = mine.shape[0]
    return pl.pallas_call(
        functools.partial(finish_kernel, len(panels)),
        grid_spec=pltpu.PrefetchScalarGridSpec(
            num_scalar_prefetch=2,
            grid=(1,),
            in_specs=[ANYWHERE] * len(panels) + [whole(a) for a in (inverse, mine, other)] + [ANYWHERE],
            out_specs=ANYWHERE,
            scratch_shapes=[
                pltpu.VMEM((2, rows + 8, width), jnp.float32),
                pltpu.VMEM((2, depth, width), jnp.float32),
                pltpu.VMEM((64, 32, depth), jnp.float32),
                pltpu.VMEM((128, 2 * width), jnp.float32),
                pltpu.VMEM((128, 2 * width), jnp.float32),
                pltpu.VMEM((2 * depth, 2 * width), jnp.bfloat16),
                pltpu.VMEM((2 * depth, 2 * width), jnp.bfloat16),
                pltpu.SemaphoreType.DMA((2,)),
                pltpu.SemaphoreType.DMA((len(panels),)),
            ],
        ),
        out_shape=jax.ShapeDtypeStruct(front.shape, jnp.float32),
        cost_estimate=pl.CostEstimate(flops=9 * 2 * 1024 * depth * 2 * width, bytes_accessed=13 * MIB, transcendentals=0),
        compiler_params=pltpu.CompilerParams(vmem_limit_bytes=32 * MIB),
        name="finish",
    )(blocks, slots, *panels, inverse, mine, other, front)


def program(right_side, pivot_inverse, ancestor_panel, ancestors, pivot_block):
    depth = pivot_inverse.shape[3]
    panel0, own_b = prepare(pivot_inverse, ancestor_panel)

    pair_a = cat([panel0, send(panel0, "yh", 1)])
    pair_b = cat([own_b, send(own_b, "yh", 1)])
    chip_a = cat([pair_a, swap(pair_a)])
    chip_b = cat([pair_b, swap(pair_b)])

    mine0, other0 = take(pivot_block, right_side, depth)
    mine0, other0 = from_owner(mine0, other0)

    x1 = send_apart(chip_a, "x", 1)
    x2 = send_apart(pair_a, "x", 2)
    own_a, other_a = pack(chip_a, [x1, swap(x1), x2, swap(x2)], (32,))

    z2 = send_apart(chip_b, "z", 2)
    z1 = send_apart(chip_b, "z", 1)
    z3 = send_apart(z2, "z", 1)
    z4 = send_apart(z2[:2], "z", 2)
    near = [z1, swap(z1), z2, swap(z2), z3, swap(z3), z4, swap(z4)]
    own_i, other_i, own_p, other_p = pack(chip_b, near, (16, 32))

    t1, o1 = send_apart(other_a, "z", 1), send_apart(own_a, "z", 1)
    t2, o2 = send_apart(t1, "z", 1), send_apart(o1, "z", 1)
    t3, o3 = send_apart(t2, "z", 1), send_apart(o2, "z", 1)
    o4 = send_apart(o3, "z", 1)
    early_a = [own_a, o1, swap(t1), o2, swap(t2)]
    late_a = [o3, swap(t3), o4]

    io1, it1 = send_apart(own_i, "x", 1), send_apart(other_i, "x", 1)
    io2 = send_apart(io1, "x", 1)
    both = [own_i, other_i, io1, it1, swap(it1), swap(io1), io2, swap(io2)]
    inverse0, inverse1 = order(both)

    po1, pt1 = send_apart(own_p, "x", 1), send_apart(other_p, "x", 1)
    po2 = send_apart(po1, "x", 1)
    panels_b = [own_p, po1, swap(pt1), po2]

    solved0 = solve(inverse0, mine0, other0)
    (early,) = project(pivot_block, ancestors[0], early_a, 0, solved0)
    sums, mine1, other1 = project(pivot_block, ancestors[0], late_a, 40, solved0, early, right_side)
    front = scatter(pivot_block, ancestors[0], right_side, sums, solved0)
    mine1, other1 = from_owner(mine1, other1)
    return finish(pivot_block, ancestors[1], panels_b, inverse1, mine1, other1, front)


def solution(mesh):
    torus = Mesh(mesh.devices.reshape(tuple(SIZES.values())), tuple(SIZES))
    in_specs = (
        P(None, ROW, SRC),
        P(None, None, SRC, None),
        P(None, None, ROW + SRC, None),
        P(None, ROW),
        P(),
    )
    return jax.shard_map(program, mesh=torus, in_specs=in_specs, out_specs=P(None, ROW, SRC), check_vma=False)
```

```python
import functools

import jax
import jax.numpy as jnp
from jax import lax
from jax.experimental import pallas as pl
from jax.experimental.pallas import tpu as pltpu
from jax.sharding import Mesh, PartitionSpec as P


SIZES = {"yh": 2, "z": 8, "x": 4, "yl": 2, "c": 2}
SRC = ("yh", "z", "x")
ROW = ("yl", "c")
MIB = 1024 * 1024
cat = jnp.concatenate


def send(value, axis, shift):
    size = SIZES[axis]
    return lax.ppermute(value, axis, [(i, (i + shift) % size) for i in range(size)])


def send_apart(value, axis, hops):
    size = SIZES[axis]
    pairs = [
        (i * 2 + core, (i + hops * (1 - 2 * core)) % size * 2 + core) for i in range(size) for core in range(2)
    ]
    return lax.ppermute(value, (axis, "c"), pairs)


def swap(value):
    return send(value, "c", 1)


def step_of(i):
    return ((i + 1) >> 1) * (1 - 2 * (i & 1))


def source(piece, x_outer):
    yh, z, x, sign = lax.axis_index("yh"), lax.axis_index("z"), lax.axis_index("x"), 1 - 2 * lax.axis_index("c")
    if x_outer:
        dx, dy, dz = step_of(piece >> 4) * sign, piece >> 3, step_of(piece & 7)
    else:
        dz, dx, dy = step_of(piece >> 3) * sign, step_of((piece >> 1) & 3), piece
    return ((yh + dy) & 1) * 32 + ((z + dz) & 7) * 4 + ((x + dx) & 3)


def owner_of(block):
    row = lax.axis_index("yl") * 2 + lax.axis_index("c")
    return block >> 2 == row, pl.multiple_of((block & 3) * 512, 512)


def prepare_kernel(inverse_ref, panel_ref, panel0_ref, own_b_ref):
    core = lax.axis_index("c")
    for node in range(2):
        own_b_ref[0, node * 8 : node * 8 + 8, :] = inverse_ref[node, core]
    for part in range(2):
        panel0_ref[0, part * 16 : part * 16 + 16, :] = panel_ref[0, part]
        own_b_ref[0, 16 + part * 16 : 32 + part * 16, :] = panel_ref[1, part]


def prepare(inverse, panel):
    depth = panel.shape[3]
    return pl.pallas_call(
        prepare_kernel,
        out_shape=[jax.ShapeDtypeStruct((1, rows, depth), jnp.float32) for rows in (32, 48)],
        compiler_params=pltpu.CompilerParams(vmem_limit_bytes=4 * MIB),
        name="prepare",
    )(inverse, panel)


def take_kernel(block_ref, front_ref, mine_ref, other_ref, rows_ref, sem):
    owned, first = owner_of(block_ref[0])
    core = lax.axis_index("c")

    @pl.when(owned)
    def _():
        copy = pltpu.make_async_copy(front_ref.at[:, pl.ds(first, rows_ref.shape[1]), :], rows_ref, sem)
        copy.start()
        copy.wait()
        mine_ref[...] = rows_ref[core]
        other_ref[...] = rows_ref[1 - core]

    @pl.when(jnp.logical_not(owned))
    def _():
        mine_ref[...] = jnp.zeros_like(mine_ref)
        other_ref[...] = jnp.zeros_like(other_ref)


def take(blocks, front, depth):
    width = front.shape[2]
    shapes = [jax.ShapeDtypeStruct((depth, width), jnp.float32)] * 2
    return pl.pallas_call(
        take_kernel,
        grid_spec=pltpu.PrefetchScalarGridSpec(
            num_scalar_prefetch=1,
            grid=(1,),
            in_specs=[ANYWHERE],
            out_specs=[whole(s) for s in shapes],
            scratch_shapes=[pltpu.VMEM((2, depth, width), jnp.float32), pltpu.SemaphoreType.DMA],
        ),
        out_shape=shapes,
        cost_estimate=pl.CostEstimate(flops=0, bytes_accessed=2 * MIB, transcendentals=0),
        compiler_params=pltpu.CompilerParams(vmem_limit_bytes=8 * MIB),
        name="take",
    )(blocks, front)


def from_owner(mine, other):
    mine = mine + swap(other)
    mine = mine + send(mine, "yl", 1)
    return mine, swap(mine)


def pack_kernel(rows, own_ref, *refs):
    pairs, outs = refs[: -2 * len(rows)], refs[-2 * len(rows) :]
    core = lax.axis_index("c")
    steps, count = len(pairs) // 2, own_ref.shape[0] // 2
    first = 0
    for which, height in enumerate(rows):
        part = slice(first, first + height)
        for who in range(2):
            out = outs[2 * which + who]
            here, there = (slice(w * count, (w + 1) * count) for w in (who, 1 - who))
            out[0] = own_ref[here, part, :]
            for k in range(1, steps):
                near, far = pairs[2 * k - 2 : 2 * k]
                out[2 * k - 1 + core] = near[here, part, :]
                out[2 * k - core] = far[there, part, :]
            out[2 * steps - 1] = pairs[2 * steps - 2 + who][:, part, :]
        first += height


def pack(own, pairs, rows):
    steps, count, depth = len(pairs), own.shape[0] // 2, own.shape[2]
    shapes = [jax.ShapeDtypeStruct((steps, count, h, depth), jnp.float32) for h in rows for _ in range(2)]
    outs = pl.pallas_call(
        functools.partial(pack_kernel, rows),
        grid=(1,),
        in_specs=[whole(a) for a in (own, *pairs)],
        out_specs=[whole(s) for s in shapes],
        out_shape=shapes,
        cost_estimate=pl.CostEstimate(flops=0, bytes_accessed=3 * MIB, transcendentals=0),
        compiler_params=pltpu.CompilerParams(vmem_limit_bytes=12 * MIB),
        name="pack",
    )(own, *pairs)
    return [out.reshape(steps * count, *out.shape[2:]) for out in outs]


def whole(array):
    return pl.BlockSpec(array.shape, lambda i, *_, n=len(array.shape): (0,) * n, pipeline_mode=pl.Buffered(1))


ANYWHERE = pl.BlockSpec(memory_space=pl.ANY)


def order_kernel(*refs):
    pieces, outs = refs[:-2], refs[-2:]
    done = 0
    for own, other in zip(pieces[::2], pieces[1::2]):
        count = own.shape[0]

        @pl.loop(0, count)
        def _(j, own=own, other=other, done=done):
            row = pl.multiple_of(source(done + j, True) * 8, 8)
            for node, out in enumerate(outs):
                out[0, pl.ds(row, 8), :] = own[j, node * 8 : node * 8 + 8, :]
                out[1, pl.ds(row, 8), :] = other[j, node * 8 : node * 8 + 8, :]

        done += count


def order(pieces):
    depth = pieces[0].shape[2]
    shapes = [jax.ShapeDtypeStruct((2, depth, depth), jnp.float32)] * 2
    return pl.pallas_call(
        order_kernel,
        grid=(1,),
        in_specs=[whole(a) for a in pieces],
        out_specs=[whole(s) for s in shapes],
        out_shape=shapes,
        cost_estimate=pl.CostEstimate(flops=0, bytes_accessed=8 * MIB, transcendentals=0),
        compiler_params=pltpu.CompilerParams(vmem_limit_bytes=12 * MIB),
        name="order",
    )(*pieces)


def split(value):
    high = value.astype(jnp.bfloat16)
    low = (value - high.astype(jnp.float32)).astype(jnp.bfloat16)
    return high, low


def put_operand(real, imag, high_ref, low_ref):
    depth, width = real.shape
    for ref, re, im in zip((high_ref, low_ref), split(real), split(imag)):
        ref[:depth, :width] = re
        ref[:depth, width:] = im
        ref[depth:, :width] = -im
        ref[depth:, width:] = re


def product(real, imag, high_ref, low_ref):
    dot = functools.partial(jnp.dot, preferred_element_type=jnp.float32)
    (re_high, re_low), (im_high, im_low) = split(real), split(imag)
    high = cat([re_high, im_high], axis=1)
    low = cat([re_low, im_low], axis=1)
    return dot(low, high_ref[...]) + dot(high, low_ref[...]) + dot(high, high_ref[...])


def solve_into(inverse_ref, mine_ref, other_ref, out_ref, high_ref, low_ref):
    width = mine_ref.shape[1]
    core = lax.axis_index("c")
    first = core == 0
    mine, other = mine_ref[...], other_ref[...]
    put_operand(jnp.where(first, mine, other), jnp.where(first, other, mine), high_ref, low_ref)

    @pl.loop(0, 2)
    def _(m):
        rows = pl.ds(pl.multiple_of(m * 256, 256), 256)
        both = product(inverse_ref[core, rows, :], inverse_ref[1 - core, rows, :], high_ref, low_ref)
        out_ref[0, rows, :] = both[:, :width]
        out_ref[1, rows, :] = both[:, width:]


def solve(inverse, mine, other):
    depth, width = mine.shape
    shape = jax.ShapeDtypeStruct((2, depth, width), jnp.float32)
    return pl.pallas_call(
        solve_into,
        grid=(1,),
        in_specs=[whole(inverse), whole(mine), whole(other)],
        out_specs=whole(shape),
        scratch_shapes=[pltpu.VMEM((2 * depth, 2 * width), jnp.bfloat16)] * 2,
        out_shape=shape,
        cost_estimate=pl.CostEstimate(flops=6 * 2 * depth * 2 * depth * 2 * width, bytes_accessed=6 * MIB, transcendentals=0),
        compiler_params=pltpu.CompilerParams(vmem_limit_bytes=24 * MIB),
        name="solve",
    )(inverse, mine, other)


def multiply_panel(part, high_ref, low_ref):
    count, depth = part.shape[0], part.shape[2]
    real = part[:, :16, :].reshape(count * 16, depth)
    imag = part[:, 16:, :].reshape(count * 16, depth)
    return product(real, imag, high_ref, low_ref)


def first_slot(slot_ref, row, last):
    low, high = jnp.int32(0), jnp.int32(last)
    for _ in range(10):
        middle = (low + high) >> 1
        slot = slot_ref[middle]
        before = (slot >= 0) & (slot < row)
        low, high = jnp.where(before, jnp.minimum(middle + 1, high), low), jnp.where(before, high, middle)
    return low


def load_pieces(refs, panel_ref, sem):
    copies, done = [], 0
    for i, ref in enumerate(refs):
        count = ref.shape[0]
        copies.append(pltpu.make_async_copy(ref, panel_ref.at[pl.ds(done, count)], sem.at[i]))
        done += count
    return copies


def project_kernel(pieces, done, first, block_ref, slot_ref, *refs):
    panel_refs = refs[:pieces]
    panel_ref, high_ref, low_ref, sem = refs[-4:]
    owned, first_row = owner_of(block_ref[1])
    copies = load_pieces(panel_refs, panel_ref, sem)
    for copy in copies:
        copy.start()
    if first:
        solved_ref, out_ref = refs[pieces : pieces + 2]
    else:
        solved_ref, so_far_ref, front_ref, out_ref, mine_ref, other_ref, sums_ref, pivot_ref, pivot_sem = refs[pieces:-4]
        depth, width = mine_ref.shape
        pivot = pltpu.make_async_copy(front_ref.at[:, pl.ds(first_row, depth), :], pivot_ref, pivot_sem)
        pivot.start()
        sums_ref[:1024, :] = so_far_ref[...]
    target_ref = out_ref if first else sums_ref
    put_operand(solved_ref[0], solved_ref[1], high_ref, low_ref)
    for copy in copies:
        copy.wait()

    @pl.loop(0, panel_ref.shape[0] // 8)
    def _(m):
        result = multiply_panel(panel_ref[pl.ds(m * 8, 8)], high_ref, low_ref)
        for j in range(8):
            row = pl.multiple_of(source(done + m * 8 + j, False) * 16, 16)
            target_ref[pl.ds(row, 16), :] = result[j * 16 : (j + 1) * 16]

    if not first:
        out_ref[...] = sums_ref[:1024, :]
        pivot.wait()

        @pl.when(owned)
        def _():
            start = first_slot(slot_ref, first_row, 1024 - depth)
            past = start & 7
            turn = (8 - past) & 7
            in_first = lax.broadcasted_iota(jnp.int32, (8, 2 * width), 0) < 8 - past
            core_first = lax.axis_index("c") == 0

            @pl.loop(0, depth // 8)
            def _(m):
                rows = pl.ds(pl.multiple_of(m * 8, 8), 8)
                base = pl.multiple_of(start - past + m * 8, 8)
                upper = pltpu.roll(sums_ref[pl.ds(base, 8), :], turn, 0)
                lower = pltpu.roll(sums_ref[pl.ds(base + 8, 8), :], turn, 0)
                taken = jnp.where(in_first, upper, lower)
                real = pivot_ref[0, rows, :] - taken[:, :width]
                imag = pivot_ref[1, rows, :] - taken[:, width:]
                mine_ref[rows, :] = jnp.where(core_first, real, imag)
                other_ref[rows, :] = jnp.where(core_first, imag, real)

        @pl.when(jnp.logical_not(owned))
        def _():
            mine_ref[...] = jnp.zeros_like(mine_ref)
            other_ref[...] = jnp.zeros_like(other_ref)


def project(blocks, slots, panels, done, solved, so_far=None, front=None):
    _, depth, width = solved.shape
    first = so_far is None
    inputs = [solved] if first else [solved, so_far]
    shapes = [jax.ShapeDtypeStruct((1024, 2 * width), jnp.float32)]
    in_specs = [ANYWHERE] * len(panels) + [whole(a) for a in inputs]
    scratch = [
        pltpu.VMEM((sum(a.shape[0] for a in panels), 32, depth), jnp.float32),
        pltpu.VMEM((2 * depth, 2 * width), jnp.bfloat16),
        pltpu.VMEM((2 * depth, 2 * width), jnp.bfloat16),
        pltpu.SemaphoreType.DMA((len(panels),)),
    ]
    if not first:
        inputs.append(front)
        in_specs.append(ANYWHERE)
        shapes += [jax.ShapeDtypeStruct((depth, width), jnp.float32)] * 2
        scratch = [
            pltpu.VMEM((1032, 2 * width), jnp.float32),
            pltpu.VMEM(solved.shape, jnp.float32),
            pltpu.SemaphoreType.DMA,
        ] + scratch
    return pl.pallas_call(
        functools.partial(project_kernel, len(panels), done, first),
        grid_spec=pltpu.PrefetchScalarGridSpec(
            num_scalar_prefetch=2,
            grid=(1,),
            in_specs=in_specs,
            out_specs=[whole(s) for s in shapes],
            scratch_shapes=scratch,
        ),
        out_shape=shapes,
        cost_estimate=pl.CostEstimate(flops=3 * 2 * 1024 * depth * 2 * width, bytes_accessed=6 * MIB, transcendentals=0),
        compiler_params=pltpu.CompilerParams(vmem_limit_bytes=24 * MIB),
        name="project",
    )(blocks, slots, *panels, *inputs)


def subtract_rows(front_ref, update_ref, first, targets):
    width = front_ref.shape[2]
    new = []
    for i, target in enumerate(targets):
        row = update_ref[pl.ds(first + i, 1), :]
        for part in range(2):
            new.append(front_ref[part, pl.ds(target, 1), :] - row[:, part * width : (part + 1) * width])
    for i, target in enumerate(targets):
        for part in range(2):
            front_ref[part, pl.ds(target, 1), :] = new[2 * i + part]


def slot_targets(slot_ref, base, count, rows):
    slots = [slot_ref[base + i] for i in range(count)]
    return [jnp.where(slot >= 0, slot, rows + i % 8) for i, slot in enumerate(slots)]


def load_front(front_ref, held_ref, sem):
    rows = front_ref.shape[1]
    return [
        pltpu.make_async_copy(front_ref.at[part], held_ref.at[part, pl.ds(0, rows), :], sem.at[part])
        for part in range(2)
    ]


def store_front(held_ref, out_ref, sem):
    rows = out_ref.shape[1]
    return [
        pltpu.make_async_copy(held_ref.at[part, pl.ds(0, rows), :], out_ref.at[part], sem.at[part])
        for part in range(2)
    ]


def scatter_kernel(block_ref, slot_ref, front_ref, update_ref, solved_ref, out_ref, held_ref, sem):
    rows, depth = front_ref.shape[1], solved_ref.shape[1]
    copies = load_front(front_ref, held_ref, sem)
    for copy in copies:
        copy.start()
    for copy in copies:
        copy.wait()

    owned, first_row = owner_of(block_ref[0])

    @pl.when(owned)
    def _():
        held_ref[:, pl.ds(first_row, depth), :] = solved_ref[...]

    @pl.loop(0, 64)
    def _(g):
        subtract_rows(held_ref, update_ref, g * 16, slot_targets(slot_ref, g * 16, 16, rows))

    copies = store_front(held_ref, out_ref, sem)
    for copy in copies:
        copy.start()
    for copy in copies:
        copy.wait()


def scatter(blocks, slots, front, update, solved):
    _, rows, width = front.shape
    return pl.pallas_call(
        scatter_kernel,
        grid_spec=pltpu.PrefetchScalarGridSpec(
            num_scalar_prefetch=2,
            grid=(1,),
            in_specs=[ANYWHERE, whole(update), whole(solved)],
            out_specs=ANYWHERE,
            scratch_shapes=[pltpu.VMEM((2, rows + 8, width), jnp.float32), pltpu.SemaphoreType.DMA((2,))],
        ),
        out_shape=jax.ShapeDtypeStruct(front.shape, jnp.float32),
        cost_estimate=pl.CostEstimate(flops=MIB, bytes_accessed=24 * MIB, transcendentals=0),
        compiler_params=pltpu.CompilerParams(vmem_limit_bytes=24 * MIB),
        name="scatter",
    )(blocks, slots, front, update, solved)


def finish_kernel(pieces, block_ref, slot_ref, *refs):
    inverse_ref, mine_ref, other_ref, front_ref, out_ref = refs[pieces : pieces + 5]
    held_ref, solved_ref, panel_ref, even_ref, odd_ref, high_ref, low_ref, front_sem, sem = refs[pieces + 5 :]
    rows = front_ref.shape[1]
    depth, _ = mine_ref.shape
    copies = load_pieces(refs[:pieces], panel_ref, sem) + load_front(front_ref, held_ref, front_sem)
    for copy in copies:
        copy.start()
    solve_into(inverse_ref, mine_ref, other_ref, solved_ref, high_ref, low_ref)
    put_operand(solved_ref[0], solved_ref[1], high_ref, low_ref)
    for copy in copies:
        copy.wait()

    owned, first_row = owner_of(block_ref[1])

    @pl.when(owned)
    def _():
        held_ref[:, pl.ds(first_row, depth), :] = solved_ref[...]

    def put_down(update_ref, m, skip=None):
        for j in range(8):
            base = source(jnp.maximum(m * 8 + j, 0), True) * 16
            targets = slot_targets(slot_ref, base, 16, rows)
            if skip is not None:
                targets = [jnp.where(skip, rows + i % 8, t) for i, t in enumerate(targets)]
            subtract_rows(held_ref, update_ref, j * 16, targets)

    @pl.loop(0, 4)
    def _(m):
        even_ref[...] = multiply_panel(panel_ref[pl.ds(m * 16, 8)], high_ref, low_ref)
        put_down(odd_ref, 2 * m - 1, skip=m == 0)
        odd_ref[...] = multiply_panel(panel_ref[pl.ds(m * 16 + 8, 8)], high_ref, low_ref)
        put_down(even_ref, 2 * m)

    put_down(odd_ref, 7)
    copies = store_front(held_ref, out_ref, front_sem)
    for copy in copies:
        copy.start()
    for copy in copies:
        copy.wait()


def finish(blocks, slots, panels, inverse, mine, other, front):
    _, rows, width = front.shape
    depth = mine.shape[0]
    return pl.pallas_call(
        functools.partial(finish_kernel, len(panels)),
        grid_spec=pltpu.PrefetchScalarGridSpec(
            num_scalar_prefetch=2,
            grid=(1,),
            in_specs=[ANYWHERE] * len(panels) + [whole(a) for a in (inverse, mine, other)] + [ANYWHERE],
            out_specs=ANYWHERE,
            scratch_shapes=[
                pltpu.VMEM((2, rows + 8, width), jnp.float32),
                pltpu.VMEM((2, depth, width), jnp.float32),
                pltpu.VMEM((64, 32, depth), jnp.float32),
                pltpu.VMEM((128, 2 * width), jnp.float32),
                pltpu.VMEM((128, 2 * width), jnp.float32),
                pltpu.VMEM((2 * depth, 2 * width), jnp.bfloat16),
                pltpu.VMEM((2 * depth, 2 * width), jnp.bfloat16),
                pltpu.SemaphoreType.DMA((2,)),
                pltpu.SemaphoreType.DMA((len(panels),)),
            ],
        ),
        out_shape=jax.ShapeDtypeStruct(front.shape, jnp.float32),
        cost_estimate=pl.CostEstimate(flops=9 * 2 * 1024 * depth * 2 * width, bytes_accessed=13 * MIB, transcendentals=0),
        compiler_params=pltpu.CompilerParams(vmem_limit_bytes=32 * MIB),
        name="finish",
    )(blocks, slots, *panels, inverse, mine, other, front)


def program(right_side, pivot_inverse, ancestor_panel, ancestors, pivot_block):
    depth = pivot_inverse.shape[3]
    panel0, own_b = prepare(pivot_inverse, ancestor_panel)

    pair_a = cat([panel0, send(panel0, "yh", 1)])
    chip_a = cat([pair_a, swap(pair_a)])
    chip_b = cat([own_b, swap(own_b)])

    mine0, other0 = take(pivot_block, right_side, depth)
    mine0, other0 = from_owner(mine0, other0)

    x1 = send_apart(chip_a, "x", 1)
    x2 = send_apart(pair_a, "x", 2)
    own_a, other_a = pack(chip_a, [x1, swap(x1), x2, swap(x2)], (32,))

    z2 = send_apart(chip_b, "z", 2)
    z1 = send_apart(chip_b, "z", 1)
    z3 = send_apart(z2, "z", 1)
    z4 = send_apart(z2[:1], "z", 2)
    near = [z1, swap(z1), z2, swap(z2), z3, swap(z3), z4, swap(z4)]
    own_i, other_i, own_p, other_p = pack(chip_b, near, (16, 32))
    across_i, across_p = send(own_i, "yh", 1), send(own_p, "yh", 1)
    own_i, other_i = cat([own_i, across_i]), cat([other_i, swap(across_i)])
    own_p, other_p = cat([own_p, across_p]), cat([other_p, swap(across_p)])

    t1, o1 = send_apart(other_a, "z", 1), send_apart(own_a, "z", 1)
    t2, o2 = send_apart(t1, "z", 1), send_apart(o1, "z", 1)
    t3, o3 = send_apart(t2, "z", 1), send_apart(o2, "z", 1)
    o4 = send_apart(o3, "z", 1)
    early_a = [own_a, o1, swap(t1), o2, swap(t2)]
    late_a = [o3, swap(t3), o4]

    io1, it1 = send_apart(own_i, "x", 1), send_apart(other_i, "x", 1)
    io2 = send_apart(io1, "x", 1)
    both = [own_i, other_i, io1, it1, swap(it1), swap(io1), io2, swap(io2)]
    inverse0, inverse1 = order(both)

    po1, pt1 = send_apart(own_p, "x", 1), send_apart(other_p, "x", 1)
    po2 = send_apart(po1, "x", 1)
    panels_b = [own_p, po1, swap(pt1), po2]

    solved0 = solve(inverse0, mine0, other0)
    (early,) = project(pivot_block, ancestors[0], early_a, 0, solved0)
    sums, mine1, other1 = project(pivot_block, ancestors[0], late_a, 40, solved0, early, right_side)
    front = scatter(pivot_block, ancestors[0], right_side, sums, solved0)
    mine1, other1 = from_owner(mine1, other1)
    return finish(pivot_block, ancestors[1], panels_b, inverse1, mine1, other1, front)


def solution(mesh):
    torus = Mesh(mesh.devices.reshape(tuple(SIZES.values())), tuple(SIZES))
    in_specs = (
        P(None, ROW, SRC),
        P(None, None, SRC, None),
        P(None, None, ROW + SRC, None),
        P(None, ROW),
        P(),
    )
    return jax.shard_map(program, mesh=torus, in_specs=in_specs, out_specs=P(None, ROW, SRC), check_vma=False)
```

```python
import functools

import jax
import jax.numpy as jnp
from jax import lax
from jax.experimental import pallas as pl
from jax.experimental.pallas import tpu as pltpu
from jax.sharding import Mesh, PartitionSpec as P


SIZES = {"yh": 2, "z": 8, "x": 4, "yl": 2, "c": 2}
SRC = ("yh", "z", "x")
ROW = ("yl", "c")
MIB = 1024 * 1024
cat = jnp.concatenate


def send(value, axis, shift):
    size = SIZES[axis]
    return lax.ppermute(value, axis, [(i, (i + shift) % size) for i in range(size)])


def send_apart(value, axis, hops):
    size = SIZES[axis]
    pairs = [
        (i * 2 + core, (i + hops * (1 - 2 * core)) % size * 2 + core) for i in range(size) for core in range(2)
    ]
    return lax.ppermute(value, (axis, "c"), pairs)


def swap(value):
    return send(value, "c", 1)


def step_of(i):
    return ((i + 1) >> 1) * (1 - 2 * (i & 1))


def source(piece, x_outer):
    yh, z, x, sign = lax.axis_index("yh"), lax.axis_index("z"), lax.axis_index("x"), 1 - 2 * lax.axis_index("c")
    if x_outer:
        dx, dy, dz = step_of(piece >> 4) * sign, piece >> 3, step_of(piece & 7)
    else:
        dz, dx, dy = step_of(piece >> 3) * sign, step_of((piece >> 1) & 3), piece
    return ((yh + dy) & 1) * 32 + ((z + dz) & 7) * 4 + ((x + dx) & 3)


def owner_of(block):
    row = lax.axis_index("yl") * 2 + lax.axis_index("c")
    return block >> 2 == row, pl.multiple_of((block & 3) * 512, 512)


def prepare_kernel(inverse_ref, panel_ref, panel0_ref, own_b_ref):
    core = lax.axis_index("c")
    for node in range(2):
        own_b_ref[0, node * 8 : node * 8 + 8, :] = inverse_ref[node, core]
    for part in range(2):
        panel0_ref[0, part * 16 : part * 16 + 16, :] = panel_ref[0, part]
        own_b_ref[0, 16 + part * 16 : 32 + part * 16, :] = panel_ref[1, part]


def prepare(inverse, panel):
    depth = panel.shape[3]
    return pl.pallas_call(
        prepare_kernel,
        out_shape=[jax.ShapeDtypeStruct((1, rows, depth), jnp.float32) for rows in (32, 48)],
        compiler_params=pltpu.CompilerParams(vmem_limit_bytes=4 * MIB),
        name="prepare",
    )(inverse, panel)


def take_kernel(block_ref, front_ref, mine_ref, other_ref, rows_ref, sem):
    owned, first = owner_of(block_ref[0])
    core = lax.axis_index("c")

    @pl.when(owned)
    def _():
        copy = pltpu.make_async_copy(front_ref.at[:, pl.ds(first, rows_ref.shape[1]), :], rows_ref, sem)
        copy.start()
        copy.wait()
        mine_ref[...] = rows_ref[core]
        other_ref[...] = rows_ref[1 - core]

    @pl.when(jnp.logical_not(owned))
    def _():
        mine_ref[...] = jnp.zeros_like(mine_ref)
        other_ref[...] = jnp.zeros_like(other_ref)


def take(blocks, front, depth):
    width = front.shape[2]
    shapes = [jax.ShapeDtypeStruct((depth, width), jnp.float32)] * 2
    return pl.pallas_call(
        take_kernel,
        grid_spec=pltpu.PrefetchScalarGridSpec(
            num_scalar_prefetch=1,
            grid=(1,),
            in_specs=[OUTSIDE],
            out_specs=[whole(s) for s in shapes],
            scratch_shapes=[pltpu.VMEM((2, depth, width), jnp.float32), pltpu.SemaphoreType.DMA],
        ),
        out_shape=shapes,
        cost_estimate=pl.CostEstimate(flops=0, bytes_accessed=2 * MIB, transcendentals=0),
        compiler_params=pltpu.CompilerParams(vmem_limit_bytes=50 * MIB),
        name="take",
    )(blocks, front)


def from_owner(mine, other):
    mine = mine + swap(other)
    mine = mine + send(mine, "yl", 1)
    return mine, swap(mine)


def pack_kernel(rows, own_ref, *refs):
    pairs, outs = refs[: -2 * len(rows)], refs[-2 * len(rows) :]
    core = lax.axis_index("c")
    steps, count = len(pairs) // 2, own_ref.shape[0] // 2
    first = 0
    for which, height in enumerate(rows):
        part = slice(first, first + height)
        for who in range(2):
            out = outs[2 * which + who]
            here, there = (slice(w * count, (w + 1) * count) for w in (who, 1 - who))
            out[0] = own_ref[here, part, :]
            for k in range(1, steps):
                near, far = pairs[2 * k - 2 : 2 * k]
                out[2 * k - 1 + core] = near[here, part, :]
                out[2 * k - core] = far[there, part, :]
            out[2 * steps - 1] = pairs[2 * steps - 2 + who][:, part, :]
        first += height


def pack(own, pairs, rows):
    steps, count, depth = len(pairs), own.shape[0] // 2, own.shape[2]
    shapes = [jax.ShapeDtypeStruct((steps, count, h, depth), jnp.float32) for h in rows for _ in range(2)]
    outs = pl.pallas_call(
        functools.partial(pack_kernel, rows),
        grid=(1,),
        in_specs=[whole(a) for a in (own, *pairs)],
        out_specs=[whole(s) for s in shapes],
        out_shape=shapes,
        cost_estimate=pl.CostEstimate(flops=0, bytes_accessed=3 * MIB, transcendentals=0),
        compiler_params=pltpu.CompilerParams(vmem_limit_bytes=12 * MIB),
        name="pack",
    )(own, *pairs)
    return [out.reshape(steps * count, *out.shape[2:]) for out in outs]


def whole(array):
    return pl.BlockSpec(array.shape, lambda i, *_, n=len(array.shape): (0,) * n, pipeline_mode=pl.Buffered(1))


ANYWHERE = pl.BlockSpec(memory_space=pl.ANY)
OUTSIDE = pl.BlockSpec(memory_space=pltpu.HBM)
INSIDE = pl.BlockSpec(memory_space=pltpu.VMEM)
SCALARS = pl.BlockSpec(memory_space=pltpu.SMEM)


def order_kernel(*refs):
    pieces, outs = refs[:-2], refs[-2:]
    done = 0
    for own, other in zip(pieces[::2], pieces[1::2]):
        count = own.shape[0]

        @pl.loop(0, count)
        def _(j, own=own, other=other, done=done):
            row = pl.multiple_of(source(done + j, True) * 8, 8)
            for node, out in enumerate(outs):
                out[0, pl.ds(row, 8), :] = own[j, node * 8 : node * 8 + 8, :]
                out[1, pl.ds(row, 8), :] = other[j, node * 8 : node * 8 + 8, :]

        done += count


def order(pieces):
    depth = pieces[0].shape[2]
    shapes = [jax.ShapeDtypeStruct((2, depth, depth), jnp.float32)] * 2
    return pl.pallas_call(
        order_kernel,
        grid=(1,),
        in_specs=[whole(a) for a in pieces],
        out_specs=[whole(s) for s in shapes],
        out_shape=shapes,
        cost_estimate=pl.CostEstimate(flops=0, bytes_accessed=8 * MIB, transcendentals=0),
        compiler_params=pltpu.CompilerParams(vmem_limit_bytes=12 * MIB),
        name="order",
    )(*pieces)


def split(value):
    high = value.astype(jnp.bfloat16)
    low = (value - high.astype(jnp.float32)).astype(jnp.bfloat16)
    return high, low


def put_operand(real, imag, high_ref, low_ref):
    depth, width = real.shape
    for ref, re, im in zip((high_ref, low_ref), split(real), split(imag)):
        ref[:depth, :width] = re
        ref[:depth, width:] = im
        ref[depth:, :width] = -im
        ref[depth:, width:] = re


def product(real, imag, high_ref, low_ref):
    dot = functools.partial(jnp.dot, preferred_element_type=jnp.float32)
    (re_high, re_low), (im_high, im_low) = split(real), split(imag)
    high = cat([re_high, im_high], axis=1)
    low = cat([re_low, im_low], axis=1)
    return dot(low, high_ref[...]) + dot(high, low_ref[...]) + dot(high, high_ref[...])


def solve_into(inverse_ref, mine_ref, other_ref, out_ref, high_ref, low_ref):
    width = mine_ref.shape[1]
    core = lax.axis_index("c")
    first = core == 0
    mine, other = mine_ref[...], other_ref[...]
    put_operand(jnp.where(first, mine, other), jnp.where(first, other, mine), high_ref, low_ref)

    @pl.loop(0, 2)
    def _(m):
        rows = pl.ds(pl.multiple_of(m * 256, 256), 256)
        both = product(inverse_ref[core, rows, :], inverse_ref[1 - core, rows, :], high_ref, low_ref)
        out_ref[0, rows, :] = both[:, :width]
        out_ref[1, rows, :] = both[:, width:]


def solve(inverse, mine, other):
    depth, width = mine.shape
    shape = jax.ShapeDtypeStruct((2, depth, width), jnp.float32)
    return pl.pallas_call(
        solve_into,
        in_specs=[INSIDE] * 3,
        out_specs=INSIDE,
        scratch_shapes=[pltpu.VMEM((2 * depth, 2 * width), jnp.bfloat16)] * 2,
        out_shape=shape,
        cost_estimate=pl.CostEstimate(flops=6 * 2 * depth * 2 * depth * 2 * width, bytes_accessed=6 * MIB, transcendentals=0),
        compiler_params=pltpu.CompilerParams(vmem_limit_bytes=24 * MIB),
        name="solve",
    )(inverse, mine, other)


def multiply_panel(part, high_ref, low_ref):
    count, depth = part.shape[0], part.shape[2]
    real = part[:, :16, :].reshape(count * 16, depth)
    imag = part[:, 16:, :].reshape(count * 16, depth)
    return product(real, imag, high_ref, low_ref)


def first_slot(slot_ref, row, last):
    low, high = jnp.int32(0), jnp.int32(last)
    for _ in range(10):
        middle = (low + high) >> 1
        slot = slot_ref[middle]
        before = (slot >= 0) & (slot < row)
        low, high = jnp.where(before, jnp.minimum(middle + 1, high), low), jnp.where(before, high, middle)
    return low


def load_pieces(refs, panel_ref, sem):
    copies, done = [], 0
    for i, ref in enumerate(refs):
        count = ref.shape[0]
        copies.append(pltpu.make_async_copy(ref, panel_ref.at[pl.ds(done, count)], sem.at[i]))
        done += count
    return copies


def project_kernel(pieces, done, first, block_ref, slot_ref, *refs):
    panel_refs = refs[:pieces]
    panel_ref, high_ref, low_ref, sem = refs[-4:]
    owned, first_row = owner_of(block_ref[1])
    copies = load_pieces(panel_refs, panel_ref, sem)
    for copy in copies:
        copy.start()
    if first:
        solved_ref, out_ref = refs[pieces : pieces + 2]
    else:
        solved_ref, so_far_ref, front_ref, out_ref, mine_ref, other_ref, sums_ref, pivot_ref, more_sem = refs[pieces:-4]
        depth, width = mine_ref.shape
        more = [
            pltpu.make_async_copy(so_far_ref, sums_ref.at[pl.ds(0, 1024)], more_sem.at[0]),
            pltpu.make_async_copy(front_ref.at[:, pl.ds(first_row, depth), :], pivot_ref, more_sem.at[1]),
        ]
        for copy in more:
            copy.start()
    put_operand(solved_ref[0], solved_ref[1], high_ref, low_ref)
    for copy in copies:
        copy.wait()

    @pl.loop(0, panel_ref.shape[0] // 8)
    def _(m):
        result = multiply_panel(panel_ref[pl.ds(m * 8, 8)], high_ref, low_ref)
        if not first:
            out_ref[pl.ds(pl.multiple_of(m * 128, 128), 128), :] = result
            return
        for j in range(8):
            row = pl.multiple_of(source(done + m * 8 + j, False) * 16, 16)
            out_ref[pl.ds(row, 16), :] = result[j * 16 : (j + 1) * 16]

    if not first:
        for copy in more:
            copy.wait()

        @pl.loop(0, panel_ref.shape[0], unroll=4)
        def _(piece):
            row = pl.multiple_of(source(done + piece, False) * 16, 16)
            sums_ref[pl.ds(row, 16), :] = out_ref[pl.ds(pl.multiple_of(piece * 16, 16), 16), :]


        @pl.when(owned)
        def _():
            start = first_slot(slot_ref, first_row, 1024 - depth)
            past = start & 7
            turn = (8 - past) & 7
            in_first = lax.broadcasted_iota(jnp.int32, (8, 2 * width), 0) < 8 - past
            core_first = lax.axis_index("c") == 0

            @pl.loop(0, depth // 8, unroll=4)
            def _(m):
                rows = pl.ds(pl.multiple_of(m * 8, 8), 8)
                base = pl.multiple_of(start - past + m * 8, 8)
                upper = pltpu.roll(sums_ref[pl.ds(base, 8), :], turn, 0)
                lower = pltpu.roll(sums_ref[pl.ds(base + 8, 8), :], turn, 0)
                taken = jnp.where(in_first, upper, lower)
                real = pivot_ref[0, rows, :] - taken[:, :width]
                imag = pivot_ref[1, rows, :] - taken[:, width:]
                mine_ref[rows, :] = jnp.where(core_first, real, imag)
                other_ref[rows, :] = jnp.where(core_first, imag, real)

        @pl.when(jnp.logical_not(owned))
        def _():
            mine_ref[...] = jnp.zeros_like(mine_ref)
            other_ref[...] = jnp.zeros_like(other_ref)


def project(blocks, slots, panels, done, solved, so_far=None, front=None):
    _, depth, width = solved.shape
    first = so_far is None
    count = sum(a.shape[0] for a in panels)
    rows = 1024 if first else count * 16
    inputs = [*panels, solved] if first else [*panels, solved, so_far, front]
    shapes = [jax.ShapeDtypeStruct((rows, 2 * width), jnp.float32)]
    scratch = [
        pltpu.VMEM((count, 32, depth), jnp.float32),
        pltpu.VMEM((2 * depth, 2 * width), jnp.bfloat16),
        pltpu.VMEM((2 * depth, 2 * width), jnp.bfloat16),
        pltpu.SemaphoreType.DMA((len(panels),)),
    ]
    if not first:
        shapes += [jax.ShapeDtypeStruct((depth, width), jnp.float32)] * 2
        scratch = [
            pltpu.VMEM((1032, 2 * width), jnp.float32),
            pltpu.VMEM(solved.shape, jnp.float32),
            pltpu.SemaphoreType.DMA((2,)),
        ] + scratch
    return pl.pallas_call(
        functools.partial(project_kernel, len(panels), done, first),
        in_specs=[SCALARS] * 2 + [ANYWHERE] * len(panels) + ([INSIDE] if first else [INSIDE, ANYWHERE, OUTSIDE]),
        out_specs=[INSIDE] * len(shapes),
        scratch_shapes=scratch,
        out_shape=shapes,
        cost_estimate=pl.CostEstimate(flops=3 * 2 * 1024 * depth * 2 * width, bytes_accessed=6 * MIB, transcendentals=0),
        compiler_params=pltpu.CompilerParams(vmem_limit_bytes=24 * MIB),
        name="project",
    )(blocks, slots, *inputs)


def subtract_rows(front_ref, update_ref, first, targets):
    width = front_ref.shape[2]
    new = []
    for i, target in enumerate(targets):
        row = update_ref[pl.ds(first + i, 1), :]
        for part in range(2):
            new.append(front_ref[part, pl.ds(target, 1), :] - row[:, part * width : (part + 1) * width])
    for i, target in enumerate(targets):
        for part in range(2):
            front_ref[part, pl.ds(target, 1), :] = new[2 * i + part]


def slot_targets(slot_ref, base, count, rows):
    slots = [slot_ref[base + i] for i in range(count)]
    return [jnp.where(slot >= 0, slot, rows + i % 8) for i, slot in enumerate(slots)]


def load_front(front_ref, held_ref, sem):
    rows = front_ref.shape[1]
    return [
        pltpu.make_async_copy(front_ref.at[part], held_ref.at[part, pl.ds(0, rows), :], sem.at[part])
        for part in range(2)
    ]


def store_front(held_ref, out_ref, sem):
    rows = out_ref.shape[1]
    return [
        pltpu.make_async_copy(held_ref.at[part, pl.ds(0, rows), :], out_ref.at[part], sem.at[part])
        for part in range(2)
    ]


def scatter_kernel(block_ref, slot_ref, front_ref, early_ref, late_ref, solved_ref, out_ref, held_ref, sem):
    rows, depth = front_ref.shape[1], solved_ref.shape[1]
    copies = load_front(front_ref, held_ref, sem)
    for copy in copies:
        copy.start()
    for copy in copies:
        copy.wait()

    owned, first_row = owner_of(block_ref[0])

    @pl.when(owned)
    def _():
        held_ref[:, pl.ds(first_row, depth), :] = solved_ref[...]

    late = late_ref.shape[0] // 16
    for first, count, update_ref in ((0, 64 - late, early_ref), (64 - late, late, late_ref)):

        @pl.loop(0, count)
        def _(piece, first=first, update_ref=update_ref):
            slot = source(first + piece, False) * 16
            place = piece if first else source(piece, False)
            targets = slot_targets(slot_ref, slot, 16, rows)
            for i in range(0, 16, 4):
                subtract_rows(held_ref, update_ref, place * 16 + i, targets[i : i + 4])

    copies = store_front(held_ref, out_ref, sem)
    for copy in copies:
        copy.start()
    for copy in copies:
        copy.wait()


def scatter(blocks, slots, front, early, late, solved):
    _, rows, width = front.shape
    return pl.pallas_call(
        scatter_kernel,
        grid_spec=pltpu.PrefetchScalarGridSpec(
            num_scalar_prefetch=2,
            grid=(1,),
            in_specs=[OUTSIDE, whole(early), whole(late), whole(solved)],
            out_specs=OUTSIDE,
            scratch_shapes=[pltpu.VMEM((2, rows + 8, width), jnp.float32), pltpu.SemaphoreType.DMA((2,))],
        ),
        out_shape=jax.ShapeDtypeStruct(front.shape, jnp.float32),
        cost_estimate=pl.CostEstimate(flops=MIB, bytes_accessed=24 * MIB, transcendentals=0),
        compiler_params=pltpu.CompilerParams(vmem_limit_bytes=24 * MIB),
        name="scatter",
    )(blocks, slots, front, early, late, solved)


def finish_kernel(pieces, block_ref, slot_ref, *refs):
    inverse_ref, mine_ref, other_ref, front_ref, out_ref = refs[pieces : pieces + 5]
    held_ref, solved_ref, panel_ref, even_ref, odd_ref, high_ref, low_ref, front_sem, sem = refs[pieces + 5 :]
    rows = front_ref.shape[1]
    depth, _ = mine_ref.shape
    copies = load_pieces(refs[:pieces], panel_ref, sem) + load_front(front_ref, held_ref, front_sem)
    for copy in copies:
        copy.start()
    solve_into(inverse_ref, mine_ref, other_ref, solved_ref, high_ref, low_ref)
    put_operand(solved_ref[0], solved_ref[1], high_ref, low_ref)
    for copy in copies:
        copy.wait()

    owned, first_row = owner_of(block_ref[1])

    @pl.when(owned)
    def _():
        held_ref[:, pl.ds(first_row, depth), :] = solved_ref[...]

    def put_down(update_ref, m, skip=None):
        for j in range(8):
            base = source(jnp.maximum(m * 8 + j, 0), True) * 16
            targets = slot_targets(slot_ref, base, 16, rows)
            if skip is not None:
                targets = [jnp.where(skip, rows + i % 8, t) for i, t in enumerate(targets)]
            for i in range(0, 16, 4):
                subtract_rows(held_ref, update_ref, j * 16 + i, targets[i : i + 4])

    @pl.loop(0, 4)
    def _(m):
        even_ref[...] = multiply_panel(panel_ref[pl.ds(m * 16, 8)], high_ref, low_ref)
        put_down(odd_ref, 2 * m - 1, skip=m == 0)
        odd_ref[...] = multiply_panel(panel_ref[pl.ds(m * 16 + 8, 8)], high_ref, low_ref)
        put_down(even_ref, 2 * m)

    put_down(odd_ref, 7)
    copies = store_front(held_ref, out_ref, front_sem)
    for copy in copies:
        copy.start()
    for copy in copies:
        copy.wait()


def finish(blocks, slots, panels, inverse, mine, other, front):
    _, rows, width = front.shape
    depth = mine.shape[0]
    return pl.pallas_call(
        functools.partial(finish_kernel, len(panels)),
        in_specs=[SCALARS] * 2 + [ANYWHERE] * len(panels) + [INSIDE] * 3 + [OUTSIDE],
        out_specs=OUTSIDE,
        scratch_shapes=[
            pltpu.VMEM((2, rows + 8, width), jnp.float32),
            pltpu.VMEM((2, depth, width), jnp.float32),
            pltpu.VMEM((64, 32, depth), jnp.float32),
            pltpu.VMEM((128, 2 * width), jnp.float32),
            pltpu.VMEM((128, 2 * width), jnp.float32),
            pltpu.VMEM((2 * depth, 2 * width), jnp.bfloat16),
            pltpu.VMEM((2 * depth, 2 * width), jnp.bfloat16),
            pltpu.SemaphoreType.DMA((2,)),
            pltpu.SemaphoreType.DMA((len(panels),)),
        ],
        out_shape=jax.ShapeDtypeStruct(front.shape, jnp.float32),
        cost_estimate=pl.CostEstimate(flops=9 * 2 * 1024 * depth * 2 * width, bytes_accessed=13 * MIB, transcendentals=0),
        compiler_params=pltpu.CompilerParams(vmem_limit_bytes=32 * MIB),
        name="finish",
    )(blocks, slots, *panels, inverse, mine, other, front)


def program(right_side, pivot_inverse, ancestor_panel, ancestors, pivot_block):
    depth = pivot_inverse.shape[3]
    panel0, own_b = prepare(pivot_inverse, ancestor_panel)

    pair_a = cat([panel0, send(panel0, "yh", 1)])
    chip_a = cat([pair_a, swap(pair_a)])
    chip_b = cat([own_b, swap(own_b)])

    mine0, other0 = take(pivot_block, right_side, depth)
    mine0, other0 = from_owner(mine0, other0)

    x1 = send_apart(chip_a, "x", 1)
    x2 = send_apart(pair_a, "x", 2)
    own_a, other_a = pack(chip_a, [x1, swap(x1), x2, swap(x2)], (32,))

    z2 = send_apart(chip_b, "z", 2)
    z1 = send_apart(chip_b, "z", 1)
    z3 = send_apart(z2, "z", 1)
    z4 = send_apart(z2[:1], "z", 2)
    near = [z1, swap(z1), z2, swap(z2), z3, swap(z3), z4, swap(z4)]
    own_i, other_i, own_p, other_p = pack(chip_b, near, (16, 32))
    across_i, across_p = send(own_i, "yh", 1), send(own_p, "yh", 1)
    own_i, other_i = cat([own_i, across_i]), cat([other_i, swap(across_i)])
    own_p, other_p = cat([own_p, across_p]), cat([other_p, swap(across_p)])

    t1, o1 = send_apart(other_a, "z", 1), send_apart(own_a, "z", 1)
    t2, o2 = send_apart(t1, "z", 1), send_apart(o1, "z", 1)
    t3, o3 = send_apart(t2, "z", 1), send_apart(o2, "z", 1)
    o4 = send_apart(o3, "z", 1)
    early_a = [own_a, o1, swap(t1), o2, swap(t2)]
    late_a = [o3, swap(t3), o4]

    io1, it1 = send_apart(own_i, "x", 1), send_apart(other_i, "x", 1)
    io2 = send_apart(io1, "x", 1)
    both = [own_i, other_i, io1, it1, swap(it1), swap(io1), io2, swap(io2)]
    inverse0, inverse1 = order(both)

    po1, pt1 = send_apart(own_p, "x", 1), send_apart(other_p, "x", 1)
    po2 = send_apart(po1, "x", 1)
    panels_b = [own_p, po1, swap(pt1), po2]

    solved0 = solve(inverse0, mine0, other0)
    (early,) = project(pivot_block, ancestors[0], early_a, 0, solved0)
    late, mine1, other1 = project(pivot_block, ancestors[0], late_a, 40, solved0, early, right_side)
    front = scatter(pivot_block, ancestors[0], right_side, early, late, solved0)
    mine1, other1 = from_owner(mine1, other1)
    return finish(pivot_block, ancestors[1], panels_b, inverse1, mine1, other1, front)


def solution(mesh):
    torus = Mesh(mesh.devices.reshape(tuple(SIZES.values())), tuple(SIZES))
    in_specs = (
        P(None, ROW, SRC),
        P(None, None, SRC, None),
        P(None, None, ROW + SRC, None),
        P(None, ROW),
        P(),
    )
    return jax.shard_map(program, mesh=torus, in_specs=in_specs, out_specs=P(None, ROW, SRC), check_vma=False)
```

```python
import functools

import jax
import jax.numpy as jnp
from jax import lax
from jax.experimental import pallas as pl
from jax.experimental.pallas import tpu as pltpu
from jax.sharding import Mesh, PartitionSpec as P


SIZES = {"yh": 2, "z": 8, "x": 4, "yl": 2, "c": 2}
SRC = ("yh", "z", "x")
ROW = ("yl", "c")
MIB = 1024 * 1024
cat = jnp.concatenate


def send(value, axis, shift):
    size = SIZES[axis]
    return lax.ppermute(value, axis, [(i, (i + shift) % size) for i in range(size)])


def send_apart(value, axis, hops):
    size = SIZES[axis]
    pairs = [
        (i * 2 + core, (i + hops * (1 - 2 * core)) % size * 2 + core) for i in range(size) for core in range(2)
    ]
    return lax.ppermute(value, (axis, "c"), pairs)


def swap(value):
    return send(value, "c", 1)


def step_of(i):
    return ((i + 1) >> 1) * (1 - 2 * (i & 1))


def source(piece, x_outer):
    yh, z, x, sign = lax.axis_index("yh"), lax.axis_index("z"), lax.axis_index("x"), 1 - 2 * lax.axis_index("c")
    if x_outer:
        dx, dy, dz = step_of(piece >> 4) * sign, piece >> 3, step_of(piece & 7)
    else:
        dz, dx, dy = step_of(piece >> 3) * sign, step_of((piece >> 1) & 3), piece
    return ((yh + dy) & 1) * 32 + ((z + dz) & 7) * 4 + ((x + dx) & 3)


def owner_of(block):
    row = lax.axis_index("yl") * 2 + lax.axis_index("c")
    return block >> 2 == row, pl.multiple_of((block & 3) * 512, 512)


def prepare_kernel(inverse_ref, panel_ref, panel0_ref, own_b_ref):
    core = lax.axis_index("c")
    for node in range(2):
        own_b_ref[0, node * 8 : node * 8 + 8, :] = inverse_ref[node, core]
    for part in range(2):
        panel0_ref[0, part * 16 : part * 16 + 16, :] = panel_ref[0, part]
        own_b_ref[0, 16 + part * 16 : 32 + part * 16, :] = panel_ref[1, part]


def prepare(inverse, panel):
    depth = panel.shape[3]
    return pl.pallas_call(
        prepare_kernel,
        out_shape=[jax.ShapeDtypeStruct((1, rows, depth), jnp.float32) for rows in (32, 48)],
        compiler_params=pltpu.CompilerParams(vmem_limit_bytes=4 * MIB),
        name="prepare",
    )(inverse, panel)


def take_kernel(block_ref, front_ref, mine_ref, other_ref, rows_ref, sem):
    owned, first = owner_of(block_ref[0])
    core = lax.axis_index("c")

    @pl.when(owned)
    def _():
        copy = pltpu.make_async_copy(front_ref.at[:, pl.ds(first, rows_ref.shape[1]), :], rows_ref, sem)
        copy.start()
        copy.wait()
        mine_ref[...] = rows_ref[core]
        other_ref[...] = rows_ref[1 - core]

    @pl.when(jnp.logical_not(owned))
    def _():
        mine_ref[...] = jnp.zeros_like(mine_ref)
        other_ref[...] = jnp.zeros_like(other_ref)


def take(blocks, front, depth):
    width = front.shape[2]
    shapes = [jax.ShapeDtypeStruct((depth, width), jnp.float32)] * 2
    return pl.pallas_call(
        take_kernel,
        grid_spec=pltpu.PrefetchScalarGridSpec(
            num_scalar_prefetch=1,
            grid=(1,),
            in_specs=[OUTSIDE],
            out_specs=[whole(s) for s in shapes],
            scratch_shapes=[pltpu.VMEM((2, depth, width), jnp.float32), pltpu.SemaphoreType.DMA],
        ),
        out_shape=shapes,
        cost_estimate=pl.CostEstimate(flops=0, bytes_accessed=2 * MIB, transcendentals=0),
        compiler_params=pltpu.CompilerParams(vmem_limit_bytes=50 * MIB),
        name="take",
    )(blocks, front)


def from_owner(mine, other):
    mine = mine + swap(other)
    mine = mine + send(mine, "yl", 1)
    return mine, swap(mine)


def pack_kernel(rows, own_ref, *refs):
    pairs, outs = refs[: -2 * len(rows)], refs[-2 * len(rows) :]
    core = lax.axis_index("c")
    steps, count = len(pairs) // 2, own_ref.shape[0] // 2
    first = 0
    for which, height in enumerate(rows):
        part = slice(first, first + height)
        for who in range(2):
            out = outs[2 * which + who]
            here, there = (slice(w * count, (w + 1) * count) for w in (who, 1 - who))
            out[0] = own_ref[here, part, :]
            for k in range(1, steps):
                near, far = pairs[2 * k - 2 : 2 * k]
                out[2 * k - 1 + core] = near[here, part, :]
                out[2 * k - core] = far[there, part, :]
            out[2 * steps - 1] = pairs[2 * steps - 2 + who][:, part, :]
        first += height


def pack(own, pairs, rows):
    steps, count, depth = len(pairs), own.shape[0] // 2, own.shape[2]
    shapes = [jax.ShapeDtypeStruct((steps, count, h, depth), jnp.float32) for h in rows for _ in range(2)]
    outs = pl.pallas_call(
        functools.partial(pack_kernel, rows),
        grid=(1,),
        in_specs=[whole(a) for a in (own, *pairs)],
        out_specs=[whole(s) for s in shapes],
        out_shape=shapes,
        cost_estimate=pl.CostEstimate(flops=0, bytes_accessed=3 * MIB, transcendentals=0),
        compiler_params=pltpu.CompilerParams(vmem_limit_bytes=12 * MIB),
        name="pack",
    )(own, *pairs)
    return [out.reshape(steps * count, *out.shape[2:]) for out in outs]


def whole(array):
    return pl.BlockSpec(array.shape, lambda i, *_, n=len(array.shape): (0,) * n, pipeline_mode=pl.Buffered(1))


ANYWHERE = pl.BlockSpec(memory_space=pl.ANY)
OUTSIDE = pl.BlockSpec(memory_space=pltpu.HBM)
INSIDE = pl.BlockSpec(memory_space=pltpu.VMEM)
SCALARS = pl.BlockSpec(memory_space=pltpu.SMEM)


def order_kernel(*refs):
    pieces, outs = refs[:-2], refs[-2:]
    done = 0
    for own, other in zip(pieces[::2], pieces[1::2]):
        count = own.shape[0]

        @pl.loop(0, count)
        def _(j, own=own, other=other, done=done):
            row = pl.multiple_of(source(done + j, True) * 8, 8)
            for node, out in enumerate(outs):
                out[0, pl.ds(row, 8), :] = own[j, node * 8 : node * 8 + 8, :]
                out[1, pl.ds(row, 8), :] = other[j, node * 8 : node * 8 + 8, :]

        done += count


def order(pieces):
    depth = pieces[0].shape[2]
    shapes = [jax.ShapeDtypeStruct((2, depth, depth), jnp.float32)] * 2
    return pl.pallas_call(
        order_kernel,
        grid=(1,),
        in_specs=[whole(a) for a in pieces],
        out_specs=[whole(s) for s in shapes],
        out_shape=shapes,
        cost_estimate=pl.CostEstimate(flops=0, bytes_accessed=8 * MIB, transcendentals=0),
        compiler_params=pltpu.CompilerParams(vmem_limit_bytes=12 * MIB),
        name="order",
    )(*pieces)


def split(value):
    high = value.astype(jnp.bfloat16)
    low = (value - high.astype(jnp.float32)).astype(jnp.bfloat16)
    return high, low


def put_operand(real, imag, high_ref, low_ref):
    depth, width = real.shape
    for ref, re, im in zip((high_ref, low_ref), split(real), split(imag)):
        ref[:depth, :width] = re
        ref[:depth, width:] = im
        ref[depth:, :width] = -im
        ref[depth:, width:] = re


def product(real, imag, high_ref, low_ref):
    dot = functools.partial(jnp.dot, preferred_element_type=jnp.float32)
    (re_high, re_low), (im_high, im_low) = split(real), split(imag)
    high = cat([re_high, im_high], axis=1)
    low = cat([re_low, im_low], axis=1)
    return dot(low, high_ref[...]) + dot(high, low_ref[...]) + dot(high, high_ref[...])


def solve_into(inverse_ref, mine_ref, other_ref, out_ref, high_ref, low_ref):
    width = mine_ref.shape[1]
    core = lax.axis_index("c")
    first = core == 0
    mine, other = mine_ref[...], other_ref[...]
    put_operand(jnp.where(first, mine, other), jnp.where(first, other, mine), high_ref, low_ref)

    @pl.loop(0, 2)
    def _(m):
        rows = pl.ds(pl.multiple_of(m * 256, 256), 256)
        both = product(inverse_ref[core, rows, :], inverse_ref[1 - core, rows, :], high_ref, low_ref)
        out_ref[0, rows, :] = both[:, :width]
        out_ref[1, rows, :] = both[:, width:]


def solve(inverse, mine, other):
    depth, width = mine.shape
    shape = jax.ShapeDtypeStruct((2, depth, width), jnp.float32)
    return pl.pallas_call(
        solve_into,
        in_specs=[INSIDE] * 3,
        out_specs=INSIDE,
        scratch_shapes=[pltpu.VMEM((2 * depth, 2 * width), jnp.bfloat16)] * 2,
        out_shape=shape,
        cost_estimate=pl.CostEstimate(flops=6 * 2 * depth * 2 * depth * 2 * width, bytes_accessed=6 * MIB, transcendentals=0),
        compiler_params=pltpu.CompilerParams(vmem_limit_bytes=24 * MIB),
        name="solve",
    )(inverse, mine, other)


def multiply_panel(part, high_ref, low_ref):
    count, depth = part.shape[0], part.shape[2]
    real = part[:, :16, :].reshape(count * 16, depth)
    imag = part[:, 16:, :].reshape(count * 16, depth)
    return product(real, imag, high_ref, low_ref)


def first_slot(slot_ref, row, last):
    low, high = jnp.int32(0), jnp.int32(last)
    for _ in range(10):
        middle = (low + high) >> 1
        slot = slot_ref[middle]
        before = (slot >= 0) & (slot < row)
        low, high = jnp.where(before, jnp.minimum(middle + 1, high), low), jnp.where(before, high, middle)
    return low


def load_pieces(refs, panel_ref, sem):
    copies, done = [], 0
    for i, ref in enumerate(refs):
        count = ref.shape[0]
        copies.append(pltpu.make_async_copy(ref, panel_ref.at[pl.ds(done, count)], sem.at[i]))
        done += count
    return copies


def project_kernel(pieces, done, first, block_ref, slot_ref, *refs):
    panel_refs = refs[:pieces]
    panel_ref, high_ref, low_ref, sem = refs[-4:]
    owned, first_row = owner_of(block_ref[1])
    copies = load_pieces(panel_refs, panel_ref, sem)
    for copy in copies:
        copy.start()
    if first:
        solved_ref, out_ref = refs[pieces : pieces + 2]
    else:
        solved_ref, so_far_ref, front_ref, out_ref, mine_ref, other_ref, sums_ref, pivot_ref, more_sem = refs[pieces:-4]
        depth, width = mine_ref.shape
        more = [
            pltpu.make_async_copy(so_far_ref, sums_ref.at[pl.ds(0, 1024)], more_sem.at[0]),
            pltpu.make_async_copy(front_ref.at[:, pl.ds(first_row, depth), :], pivot_ref, more_sem.at[1]),
        ]
        for copy in more:
            copy.start()
    put_operand(solved_ref[0], solved_ref[1], high_ref, low_ref)
    for copy in copies:
        copy.wait()

    @pl.loop(0, panel_ref.shape[0] // 8)
    def _(m):
        result = multiply_panel(panel_ref[pl.ds(m * 8, 8)], high_ref, low_ref)
        if not first:
            out_ref[pl.ds(pl.multiple_of(m * 128, 128), 128), :] = result
            return
        for j in range(8):
            row = pl.multiple_of(source(done + m * 8 + j, False) * 16, 16)
            out_ref[pl.ds(row, 16), :] = result[j * 16 : (j + 1) * 16]

    if not first:
        for copy in more:
            copy.wait()

        @pl.loop(0, panel_ref.shape[0], unroll=4)
        def _(piece):
            row = pl.multiple_of(source(done + piece, False) * 16, 16)
            sums_ref[pl.ds(row, 16), :] = out_ref[pl.ds(pl.multiple_of(piece * 16, 16), 16), :]


        @pl.when(owned)
        def _():
            start = first_slot(slot_ref, first_row, 1024 - depth)
            past = start & 7
            turn = (8 - past) & 7
            in_first = lax.broadcasted_iota(jnp.int32, (8, 2 * width), 0) < 8 - past
            core_first = lax.axis_index("c") == 0

            @pl.loop(0, depth // 8, unroll=4)
            def _(m):
                rows = pl.ds(pl.multiple_of(m * 8, 8), 8)
                base = pl.multiple_of(start - past + m * 8, 8)
                upper = pltpu.roll(sums_ref[pl.ds(base, 8), :], turn, 0)
                lower = pltpu.roll(sums_ref[pl.ds(base + 8, 8), :], turn, 0)
                taken = jnp.where(in_first, upper, lower)
                real = pivot_ref[0, rows, :] - taken[:, :width]
                imag = pivot_ref[1, rows, :] - taken[:, width:]
                mine_ref[rows, :] = jnp.where(core_first, real, imag)
                other_ref[rows, :] = jnp.where(core_first, imag, real)

        @pl.when(jnp.logical_not(owned))
        def _():
            mine_ref[...] = jnp.zeros_like(mine_ref)
            other_ref[...] = jnp.zeros_like(other_ref)


def project(blocks, slots, panels, done, solved, so_far=None, front=None):
    _, depth, width = solved.shape
    first = so_far is None
    count = sum(a.shape[0] for a in panels)
    rows = 1024 if first else count * 16
    inputs = [*panels, solved] if first else [*panels, solved, so_far, front]
    shapes = [jax.ShapeDtypeStruct((rows, 2 * width), jnp.float32)]
    scratch = [
        pltpu.VMEM((count, 32, depth), jnp.float32),
        pltpu.VMEM((2 * depth, 2 * width), jnp.bfloat16),
        pltpu.VMEM((2 * depth, 2 * width), jnp.bfloat16),
        pltpu.SemaphoreType.DMA((len(panels),)),
    ]
    if not first:
        shapes += [jax.ShapeDtypeStruct((depth, width), jnp.float32)] * 2
        scratch = [
            pltpu.VMEM((1032, 2 * width), jnp.float32),
            pltpu.VMEM(solved.shape, jnp.float32),
            pltpu.SemaphoreType.DMA((2,)),
        ] + scratch
    return pl.pallas_call(
        functools.partial(project_kernel, len(panels), done, first),
        in_specs=[SCALARS] * 2 + [ANYWHERE] * len(panels) + ([INSIDE] if first else [INSIDE, ANYWHERE, OUTSIDE]),
        out_specs=[INSIDE] * len(shapes),
        scratch_shapes=scratch,
        out_shape=shapes,
        cost_estimate=pl.CostEstimate(flops=3 * 2 * 1024 * depth * 2 * width, bytes_accessed=6 * MIB, transcendentals=0),
        compiler_params=pltpu.CompilerParams(vmem_limit_bytes=24 * MIB),
        name="project",
    )(blocks, slots, *inputs)


def subtract_rows(front_ref, update_ref, first, targets):
    width = front_ref.shape[2]
    new = []
    for i, target in enumerate(targets):
        row = update_ref[pl.ds(first + i, 1), :]
        for part in range(2):
            new.append(front_ref[part, pl.ds(target, 1), :] - row[:, part * width : (part + 1) * width])
    for i, target in enumerate(targets):
        for part in range(2):
            front_ref[part, pl.ds(target, 1), :] = new[2 * i + part]


def slot_targets(slot_ref, base, count, rows):
    slots = [slot_ref[base + i] for i in range(count)]
    return [jnp.where(slot >= 0, slot, rows + i % 8) for i, slot in enumerate(slots)]


def load_front(front_ref, held_ref, sem):
    rows = front_ref.shape[1]
    return [
        pltpu.make_async_copy(front_ref.at[part], held_ref.at[part, pl.ds(0, rows), :], sem.at[part])
        for part in range(2)
    ]


def store_front(held_ref, out_ref, sem):
    rows = out_ref.shape[1]
    return [
        pltpu.make_async_copy(held_ref.at[part, pl.ds(0, rows), :], out_ref.at[part], sem.at[part])
        for part in range(2)
    ]


def scatter_kernel(block_ref, slot_ref, front_ref, early_ref, late_ref, solved_ref, out_ref, held_ref, sem):
    rows, depth = front_ref.shape[1], solved_ref.shape[1]
    copies = load_front(front_ref, held_ref, sem)
    for copy in copies:
        copy.start()
    for copy in copies:
        copy.wait()

    owned, first_row = owner_of(block_ref[0])

    @pl.when(owned)
    def _():
        held_ref[:, pl.ds(first_row, depth), :] = solved_ref[...]

    late = late_ref.shape[0] // 16
    for first, count, update_ref in ((0, 64 - late, early_ref), (64 - late, late, late_ref)):

        @pl.loop(0, count)
        def _(piece, first=first, update_ref=update_ref):
            slot = source(first + piece, False) * 16
            place = piece if first else source(piece, False)
            targets = slot_targets(slot_ref, slot, 16, rows)
            for i in range(0, 16, 2):
                subtract_rows(held_ref, update_ref, place * 16 + i, targets[i : i + 2])

    copies = store_front(held_ref, out_ref, sem)
    for copy in copies:
        copy.start()
    for copy in copies:
        copy.wait()


def scatter(blocks, slots, front, early, late, solved):
    _, rows, width = front.shape
    return pl.pallas_call(
        scatter_kernel,
        grid_spec=pltpu.PrefetchScalarGridSpec(
            num_scalar_prefetch=2,
            grid=(1,),
            in_specs=[OUTSIDE, whole(early), whole(late), whole(solved)],
            out_specs=OUTSIDE,
            scratch_shapes=[pltpu.VMEM((2, rows + 8, width), jnp.float32), pltpu.SemaphoreType.DMA((2,))],
        ),
        out_shape=jax.ShapeDtypeStruct(front.shape, jnp.float32),
        cost_estimate=pl.CostEstimate(flops=MIB, bytes_accessed=24 * MIB, transcendentals=0),
        compiler_params=pltpu.CompilerParams(vmem_limit_bytes=24 * MIB),
        name="scatter",
    )(blocks, slots, front, early, late, solved)


def finish_kernel(pieces, block_ref, slot_ref, *refs):
    inverse_ref, mine_ref, other_ref, front_ref, out_ref = refs[pieces : pieces + 5]
    held_ref, solved_ref, panel_ref, even_ref, odd_ref, high_ref, low_ref, front_sem, sem = refs[pieces + 5 :]
    rows = front_ref.shape[1]
    depth, _ = mine_ref.shape
    copies = load_pieces(refs[:pieces], panel_ref, sem) + load_front(front_ref, held_ref, front_sem)
    for copy in copies:
        copy.start()
    solve_into(inverse_ref, mine_ref, other_ref, solved_ref, high_ref, low_ref)
    put_operand(solved_ref[0], solved_ref[1], high_ref, low_ref)
    for copy in copies:
        copy.wait()

    owned, first_row = owner_of(block_ref[1])

    @pl.when(owned)
    def _():
        held_ref[:, pl.ds(first_row, depth), :] = solved_ref[...]

    def put_down(update_ref, m, skip=None):
        for j in range(8):
            base = source(jnp.maximum(m * 8 + j, 0), True) * 16
            targets = slot_targets(slot_ref, base, 16, rows)
            if skip is not None:
                targets = [jnp.where(skip, rows + i % 8, t) for i, t in enumerate(targets)]
            for i in range(0, 16, 2):
                subtract_rows(held_ref, update_ref, j * 16 + i, targets[i : i + 2])

    @pl.loop(0, 4)
    def _(m):
        even_ref[...] = multiply_panel(panel_ref[pl.ds(m * 16, 8)], high_ref, low_ref)
        put_down(odd_ref, 2 * m - 1, skip=m == 0)
        odd_ref[...] = multiply_panel(panel_ref[pl.ds(m * 16 + 8, 8)], high_ref, low_ref)
        put_down(even_ref, 2 * m)

    put_down(odd_ref, 7)
    copies = store_front(held_ref, out_ref, front_sem)
    for copy in copies:
        copy.start()
    for copy in copies:
        copy.wait()


def finish(blocks, slots, panels, inverse, mine, other, front):
    _, rows, width = front.shape
    depth = mine.shape[0]
    return pl.pallas_call(
        functools.partial(finish_kernel, len(panels)),
        in_specs=[SCALARS] * 2 + [ANYWHERE] * len(panels) + [INSIDE] * 3 + [OUTSIDE],
        out_specs=OUTSIDE,
        scratch_shapes=[
            pltpu.VMEM((2, rows + 8, width), jnp.float32),
            pltpu.VMEM((2, depth, width), jnp.float32),
            pltpu.VMEM((64, 32, depth), jnp.float32),
            pltpu.VMEM((128, 2 * width), jnp.float32),
            pltpu.VMEM((128, 2 * width), jnp.float32),
            pltpu.VMEM((2 * depth, 2 * width), jnp.bfloat16),
            pltpu.VMEM((2 * depth, 2 * width), jnp.bfloat16),
            pltpu.SemaphoreType.DMA((2,)),
            pltpu.SemaphoreType.DMA((len(panels),)),
        ],
        out_shape=jax.ShapeDtypeStruct(front.shape, jnp.float32),
        cost_estimate=pl.CostEstimate(flops=9 * 2 * 1024 * depth * 2 * width, bytes_accessed=13 * MIB, transcendentals=0),
        compiler_params=pltpu.CompilerParams(vmem_limit_bytes=32 * MIB),
        name="finish",
    )(blocks, slots, *panels, inverse, mine, other, front)


def program(right_side, pivot_inverse, ancestor_panel, ancestors, pivot_block):
    depth = pivot_inverse.shape[3]
    panel0, own_b = prepare(pivot_inverse, ancestor_panel)

    pair_a = cat([panel0, send(panel0, "yh", 1)])
    chip_a = cat([pair_a, swap(pair_a)])
    chip_b = cat([own_b, swap(own_b)])

    mine0, other0 = take(pivot_block, right_side, depth)
    mine0, other0 = from_owner(mine0, other0)

    x1 = send_apart(chip_a, "x", 1)
    x2 = send_apart(pair_a, "x", 2)
    own_a, other_a = pack(chip_a, [x1, swap(x1), x2, swap(x2)], (32,))

    z2 = send_apart(chip_b, "z", 2)
    z1 = send_apart(chip_b, "z", 1)
    z3 = send_apart(z2, "z", 1)
    z4 = send_apart(z2[:1], "z", 2)
    near = [z1, swap(z1), z2, swap(z2), z3, swap(z3), z4, swap(z4)]
    own_i, other_i, own_p, other_p = pack(chip_b, near, (16, 32))
    across_i, across_p = send(own_i, "yh", 1), send(own_p, "yh", 1)
    own_i, other_i = cat([own_i, across_i]), cat([other_i, swap(across_i)])
    own_p, other_p = cat([own_p, across_p]), cat([other_p, swap(across_p)])

    t1, o1 = send_apart(other_a, "z", 1), send_apart(own_a, "z", 1)
    t2, o2 = send_apart(t1, "z", 1), send_apart(o1, "z", 1)
    t3, o3 = send_apart(t2, "z", 1), send_apart(o2, "z", 1)
    o4 = send_apart(o3, "z", 1)
    early_a = [own_a, o1, swap(t1), o2, swap(t2)]
    late_a = [o3, swap(t3), o4]

    io1, it1 = send_apart(own_i, "x", 1), send_apart(other_i, "x", 1)
    io2 = send_apart(io1, "x", 1)
    both = [own_i, other_i, io1, it1, swap(it1), swap(io1), io2, swap(io2)]
    inverse0, inverse1 = order(both)

    po1, pt1 = send_apart(own_p, "x", 1), send_apart(other_p, "x", 1)
    po2 = send_apart(po1, "x", 1)
    panels_b = [own_p, po1, swap(pt1), po2]

    solved0 = solve(inverse0, mine0, other0)
    (early,) = project(pivot_block, ancestors[0], early_a, 0, solved0)
    late, mine1, other1 = project(pivot_block, ancestors[0], late_a, 40, solved0, early, right_side)
    front = scatter(pivot_block, ancestors[0], right_side, early, late, solved0)
    mine1, other1 = from_owner(mine1, other1)
    return finish(pivot_block, ancestors[1], panels_b, inverse1, mine1, other1, front)


def solution(mesh):
    torus = Mesh(mesh.devices.reshape(tuple(SIZES.values())), tuple(SIZES))
    in_specs = (
        P(None, ROW, SRC),
        P(None, None, SRC, None),
        P(None, None, ROW + SRC, None),
        P(None, ROW),
        P(),
    )
    return jax.shard_map(program, mesh=torus, in_specs=in_specs, out_specs=P(None, ROW, SRC), check_vma=False)
```
